32 devices in a mesh: groups: 2 (over y), seq: 4 (over z), blk: 2 (over x), hd: 2 (over core).
Axes of the slice: x: 2, y: 2, z: 4, core: 2. Of those that a mesh axis runs over, the one named last changes fastest.
Arguments:
- query_raw: bfloat16 [8192, 2048], P(('groups', 'seq', 'blk'), 'hd'), parts along dimension 0, may hold values from -6 to 6
- key_raw: bfloat16 [8192, 2048], P(('groups', 'seq', 'blk'), 'hd'), parts along dimension 0, may hold values from -6 to 6
- value_raw: bfloat16 [8192, 2048], P(('groups', 'seq', 'blk'), 'hd'), parts along dimension 0, may hold values from -6 to 6
- beta_rate: float32 [8192, 16], P(('groups', 'seq', 'blk'), 'hd'), parts along dimension 0, may hold values from 0 to 1
- conv_weight: float32 [3, 4, 2048], P(None, None, 'hd'), may hold values from -3 to 3
- out_gain: float32 [128], replicated, may hold values from 0.1 to 1.9
Outputs:
- head_output: bfloat16 [8192, 2048], P(('groups', 'seq', 'blk'), 'hd'), parts along dimension 0
The draws below stay inside these ranges and needn't reach their ends.
There are 2 independent parts, one for each index of `groups`. The reference program is written for one: setup_inputs(seed, part) draws one part's arguments, and reference() takes and returns one part's arrays. A program takes and returns all parts, laid end to end along the dimension named above; an argument that names none is the same for every part. Nothing has to cross between parts.
All inputs are finite; a program needn't handle non-finite values.
Results may differ from the reference program's by a relative error of at most 0.0064.
Values may be sent and summed in bfloat16 or wider, within the bound.
A program may use at most 192 MiB of HBM per device.

```python
import math
import jax
import jax.numpy as jnp
from jax import lax

HEADS = 16
KEY_SIZE = 128
DV = 128
CONV = 4
SPAN = 64
TOKEN_TOTAL = 4096


def draw_beta_rate(key, part):
    random_subkeys = jax.random.split(key, 6)
    token_positions = jnp.arange(TOKEN_TOTAL)
    fast_share = 0.5
    fast_heads = jax.random.uniform(random_subkeys[0], (HEADS,)) < fast_share
    fast_rate = jnp.exp(jax.random.uniform(random_subkeys[1], (HEADS,), minval=math.log(0.3), maxval=math.log(0.9)))
    slow_rate = jnp.exp(jax.random.uniform(random_subkeys[2], (HEADS,), minval=math.log(0.01), maxval=math.log(0.1)))
    base_rate = jnp.where(fast_heads, fast_rate, slow_rate)
    roughness = jnp.exp(jax.random.uniform(random_subkeys[3], (TOKEN_TOTAL, HEADS), minval=-math.log(2.0), maxval=math.log(2.0)))
    segment_count = TOKEN_TOTAL // 128 + 1
    segment_factor = jnp.exp(jax.random.uniform(random_subkeys[4], (segment_count, HEADS), minval=-math.log(2.0), maxval=math.log(2.0)))
    spread = segment_factor[token_positions // 128]
    segment_length = max(KEY_SIZE * 3 // 8, 1)
    segment_starts = jax.random.randint(random_subkeys[5], (3,), 0, TOKEN_TOTAL - segment_length)
    within_segment = jnp.any((token_positions[:, None] >= segment_starts[None, :]) & (token_positions[:, None] < segment_starts[None, :] + segment_length), axis=1)
    strength = jnp.minimum(base_rate[None, :] * roughness * spread, 1.0)
    return jnp.where(within_segment[:, None], 0.9, strength).astype(jnp.float32)


def shard_levels(rng, dims, cuts, least, largest):
    factor_of = 1.0
    for dim, shards_of in cuts:
        heights = jax.random.uniform(jax.random.fold_in(jax.random.fold_in(rng, 6), dim), (shards_of,), jnp.float32, least / len(cuts), largest / len(cuts))
        factor_of = factor_of * jnp.repeat(jnp.exp(heights), dims[dim] // shards_of).reshape((-1,) + (1,) * (len(dims) - 1 - dim))
    return factor_of


def bell_draw(stream_key, shape, scale, most, pieces=(), kind=jnp.bfloat16):
    entries = scale * jax.random.normal(stream_key, shape, jnp.float32)
    if pieces:
        entries = entries * shard_levels(stream_key, shape, pieces, -0.22, 0.18)
    return jnp.clip(entries, -most, most).astype(kind)


def setup_inputs(seed: int = 0, part: int = 0) -> dict:
    streams_of = jax.random.split(jax.random.key(seed), 7)
    part_keys = jax.random.split(jax.random.fold_in(streams_of[6], part), 7)
    query_raw = bell_draw(part_keys[0], (TOKEN_TOTAL, HEADS * KEY_SIZE), 1.0, 6.0, ((0, 8), (1, 2)))
    key_raw = bell_draw(part_keys[1], (TOKEN_TOTAL, HEADS * KEY_SIZE), 1.0, 6.0, ((0, 8), (1, 2)))
    value_raw = bell_draw(part_keys[2], (TOKEN_TOTAL, HEADS * DV), 1.0, 6.0, ((0, 8), (1, 2)))
    beta_rate = draw_beta_rate(jax.random.fold_in(jax.random.fold_in(streams_of[6], part), 71), part)
    conv_weight = bell_draw(streams_of[4], (3, CONV, HEADS * KEY_SIZE), CONV ** -0.5, 3.0, ((2, 2),), jnp.float32)
    out_gain = jnp.clip(1.0 + 0.18 * jax.random.normal(streams_of[5], (DV,), jnp.float32), 0.1, 1.9)
    return {"query_raw": query_raw, "key_raw": key_raw, "value_raw": value_raw, "beta_rate": beta_rate, "conv_weight": conv_weight, "out_gain": out_gain}


PRECISE = lax.Precision.HIGHEST

def short_conv(raw, weights):
    kernel_len = weights.shape[0]
    tok_rows = raw.shape[0]
    padded = jnp.pad(raw.astype(jnp.float32), ((kernel_len - 1, 0), (0, 0)))
    summed = jnp.zeros(raw.shape, jnp.float32)
    for offset in range(kernel_len):
        summed = summed + weights[offset] * padded[offset:offset + tok_rows]
    return jax.nn.silu(summed)

def reference(query_raw, key_raw, value_raw, beta_rate, conv_weight, out_gain):
    queries = short_conv(query_raw, conv_weight[0]).astype(jnp.bfloat16)
    conv_k = short_conv(key_raw, conv_weight[1]).reshape(TOKEN_TOTAL, HEADS, KEY_SIZE)
    keys_norm = (conv_k * lax.rsqrt(lax.optimization_barrier(jnp.sum(conv_k * conv_k, axis=-1, keepdims=True)) + 1e-06)).astype(jnp.bfloat16)
    values = short_conv(value_raw, conv_weight[2]).astype(jnp.bfloat16)
    span_count = TOKEN_TOTAL // SPAN
    q_blocks = jnp.transpose(queries.reshape(span_count, SPAN, HEADS, KEY_SIZE), (0, 2, 1, 3))
    k_blocks = jnp.transpose(keys_norm.reshape(span_count, SPAN, HEADS, KEY_SIZE), (0, 2, 1, 3))
    v_blocks = jnp.transpose(values.reshape(span_count, SPAN, HEADS, DV), (0, 2, 1, 3))
    rate_blocks = jnp.transpose(beta_rate.reshape(span_count, SPAN, HEADS), (0, 2, 1))
    row_index = lax.broadcasted_iota(jnp.int32, (SPAN, SPAN), 0)
    col_index = lax.broadcasted_iota(jnp.int32, (SPAN, SPAN), 1)
    unit_span = jnp.eye(SPAN, dtype=jnp.float32)

    def advance(carry_state, inputs):
        query_part, key_part, value_part, rate_part = inputs
        query_part = query_part.astype(jnp.float32)
        key_part = key_part.astype(jnp.float32)
        value_part = value_part.astype(jnp.float32)
        key_gram = jnp.einsum('hcd,hsd->hcs', key_part, key_part, precision=PRECISE)
        scores = jnp.einsum('hcd,hsd->hcs', query_part, key_part, precision=PRECISE)
        system = unit_span + jnp.where(col_index < row_index, rate_part[:, :, None] * key_gram, 0.0)
        right_side = rate_part[:, :, None] * jnp.concatenate((key_part, value_part), axis=-1)
        solved = jax.scipy.linalg.solve_triangular(system, right_side, lower=True, unit_diagonal=True)
        w_factor = solved[..., :KEY_SIZE]
        u_factor = solved[..., KEY_SIZE:]
        corrected = u_factor - jnp.einsum('hcd,hde->hce', w_factor, carry_state, precision=PRECISE)
        masked = jnp.where(col_index <= row_index, scores, 0.0)
        result = jnp.einsum('hcd,hde->hce', query_part, carry_state, precision=PRECISE)
        result = result + jnp.einsum('hcs,hse->hce', masked, corrected, precision=PRECISE)
        carry_state = carry_state + jnp.einsum('hcd,hce->hde', key_part, corrected, precision=PRECISE)
        return (carry_state, result)
    start_state = jnp.zeros((HEADS, KEY_SIZE, DV), jnp.float32)
    last_state, span_out = lax.scan(advance, start_state, (q_blocks, k_blocks, v_blocks, rate_blocks))
    mean_sq = lax.optimization_barrier(jnp.mean(span_out * span_out, axis=-1, keepdims=True))
    normed = span_out * lax.rsqrt(mean_sq + 1e-05) * out_gain
    return jnp.transpose(normed, (0, 2, 1, 3)).reshape(TOKEN_TOTAL, HEADS * DV).astype(jnp.bfloat16)
```

```python
import functools

import jax
import jax.numpy as jnp
from jax import lax
from jax.experimental import pallas as pl
from jax.experimental.pallas import tpu as pltpu
from jax.sharding import PartitionSpec as P

F32 = jnp.float32
BF16 = jnp.bfloat16
CHUNK = 128
RIM = 16
LEAD = 8
PAIR = 4
SMALL = 16
MESH = pl.DeviceIdType.MESH


def mm(a, b):
    return jnp.dot(a.astype(BF16), b.astype(BF16), preferred_element_type=F32)


def mm_nt(a, b):
    return lax.dot_general(a, b, (((1,), (1,)), ((), ())), preferred_element_type=F32)


def stack(parts, axis=0):
    return jnp.concatenate(parts, axis=axis)


def each(lefts, rights):
    made = []
    for i in range(0, len(lefts), 2):
        rows, cols = lefts[i].shape[0], rights[i].shape[1]
        both = mm(stack(lefts[i:i + 2]), stack(rights[i:i + 2], axis=1))
        made += [both[:rows, :cols], both[rows:, cols:]]
    return made


def layer_kernel(seqs, blks, taps, q_hbm, k_hbm, v_hbm, w_hbm, beta_hbm, gain_hbm, o_ref,
                 raw, rim, pad, keys, w_ref, beta_ref, gain_ref, wu_ref, state_ref, ab_ref, lead_ref,
                 known_ref, came, goes, before, onward, row_a, row_b, load_sem, small_sem, rim_send,
                 rim_recv, join_send, join_recv, send_sem, recv_sem):
    rows = q_hbm.shape[0]
    heads, dim = ab_ref.shape[0], ab_ref.shape[1]
    chunks = rows // CHUNK
    pairs = heads // PAIR
    total = seqs * blks
    z, x = lax.axis_index("seq"), lax.axis_index("blk")
    end = blks - 1
    here = z * blks + x
    lag = z + end
    sends_row = x < end
    sends_state = (x == end) & (z < seqs - 1)
    below = (z + 1) % seqs
    after = (here + 1) % total
    ahead = (here + total - 1) % total
    after_id = {"seq": after // blks, "blk": after % blks}
    ahead_id = {"seq": ahead // blks, "blk": ahead % blks}
    has_ahead = here > 0
    has_after = here < total - 1
    sources = (q_hbm, k_hbm, v_hbm)
    smalls = ((w_hbm, w_ref), (beta_hbm, beta_ref), (gain_hbm, gain_ref))

    def load(which):
        return pltpu.make_async_copy(sources[which], raw.at[which], load_sem.at[which])

    def load_small(i):
        return pltpu.make_async_copy(smalls[i][0], smalls[i][1], small_sem.at[i])

    def rim_move(which):
        return pltpu.make_async_remote_copy(
            src_ref=sources[which].at[pl.ds(rows - RIM, RIM)], dst_ref=rim.at[which],
            send_sem=rim_send.at[which], recv_sem=rim_recv.at[which],
            device_id=after_id, device_id_type=MESH)

    def join(head):
        return pltpu.make_async_remote_copy(
            src_ref=onward.at[head], dst_ref=before.at[head],
            send_sem=join_send.at[head], recv_sem=join_recv.at[head],
            device_id={"seq": z, "blk": (x + 1) % blks}, device_id_type=MESH)

    def move(head, target):
        return pltpu.make_async_remote_copy(
            src_ref=goes.at[head], dst_ref=came.at[head],
            send_sem=send_sem.at[target, head], recv_sem=recv_sem.at[head],
            device_id={"seq": below, "blk": target}, device_id_type=MESH)

    barrier = pltpu.get_barrier_semaphore()

    @pl.when(has_ahead)
    def _():
        pl.semaphore_signal(barrier, inc=1, device_id=ahead_id, device_id_type=MESH)

    @pl.when(has_after)
    def _():
        pl.semaphore_signal(barrier, inc=1, device_id=after_id, device_id_type=MESH)

    load(1).start()
    load_small(0).start()
    load_small(1).start()
    load(2).start()
    load(0).start()
    load_small(2).start()

    @pl.when(here == 0)
    def _():
        rim[...] = jnp.zeros_like(rim)

    @pl.when(z == 0)
    def _():
        came[...] = jnp.zeros_like(came)

    @pl.when(x == 0)
    def _():
        before[...] = jnp.zeros_like(before)

    extra_up = (x > 0) & (z > 0)

    @pl.when(extra_up)
    def _():
        pl.semaphore_signal(barrier, inc=1, device_id={"seq": (z + seqs - 1) % seqs, "blk": end},
                            device_id_type=MESH)

    @pl.when(sends_state)
    def _():
        for target in range(1, blks):
            pl.semaphore_signal(barrier, inc=1, device_id={"seq": below, "blk": target},
                                device_id_type=MESH)

    pl.semaphore_wait(
        barrier,
        has_ahead.astype(jnp.int32) + has_after.astype(jnp.int32)
        + extra_up.astype(jnp.int32) + end * sends_state.astype(jnp.int32))

    @pl.when(has_after)
    def _():
        for which in (1, 2, 0):
            rim_move(which).start()

    def arrive(which):
        load(which).wait()

        @pl.when(has_ahead)
        def _():
            rim_move(which).wait_recv()

    load_small(0).wait()
    load_small(1).wait()
    load_small(2).wait()
    arrive(1)
    arrive(2)

    row = lax.broadcasted_iota(jnp.int32, (CHUNK, CHUNK), 0)
    col = lax.broadcasted_iota(jnp.int32, (CHUNK, CHUNK), 1)
    head_row = lax.broadcasted_iota(jnp.int32, (heads, CHUNK), 0)
    lane = lax.broadcasted_iota(jnp.int32, (SMALL, CHUNK), 1)
    level = lax.broadcasted_iota(jnp.int32, (SMALL, CHUNK), 0)

    def keep(mask):
        return jnp.where(mask, 1.0, 0.0).astype(BF16)

    unit = jnp.where(lane % SMALL == level, 1.0, 0.0)
    spots = {}
    size = SMALL
    while size < CHUNK:
        spots[size] = [keep(lane // size == i) for i in range(CHUNK // size)]
        size *= 2
    evens = {s: keep(lane // s % 2 == 0) for s in spots}
    odds = {s: keep(lane // s % 2 == 1) for s in spots}

    def masked(x, mask):
        return stack([x[i:i + SMALL] * mask for i in range(0, x.shape[0], SMALL)])

    def lanes_of(head):
        return pl.ds(pl.multiple_of(head * dim, dim), dim)

    def conv(which, head, slot):
        lanes = lanes_of(head)
        pad[slot, 0:LEAD] = rim[which, RIM - LEAD:RIM, lanes].astype(F32)
        pad[slot, LEAD:] = raw[which, :, lanes].astype(F32)
        half = None
        for tap in range(taps):
            term = (0.5 * w_ref[which, tap:tap + 1, lanes]) * pad[
                slot, pl.ds(LEAD - taps + 1 + tap, rows)]
            half = term if half is None else half + term
        return half + half * jnp.tanh(half)

    def maps_of(pair):
        ks, vs, turned, flat, system = [], [], [], [], []
        for lane_of in range(PAIR):
            head = pair * PAIR + lane_of
            k = conv(1, head, lane_of * 2)
            k = (k * lax.rsqrt(jnp.sum(k * k, axis=-1, keepdims=True) + 1e-06)).astype(BF16)
            v = conv(2, head, lane_of * 2 + 1).astype(BF16)
            for c in range(chunks):
                part = slice(c * CHUNK, (c + 1) * CHUNK)
                ks.append(k[part])
                turned.append(k[part].T)
                keys[head, part] = turned[-1]
                vs.append(v[part])
                flat.append(jnp.sum(jnp.where(head_row == head, beta_ref[:, part], 0.0), axis=0, keepdims=True))
        for k, kt, f in zip(ks, turned, flat):
            down = jnp.sum(jnp.where(row == col, -f, 0.0), axis=1, keepdims=True)
            system.append(jnp.where(col < row, down * mm(k, kt), 0.0).astype(BF16))
        near = [[x[i * SMALL:(i + 1) * SMALL] * m for i, m in enumerate(spots[SMALL])] for x in system]
        power = [functools.reduce(lambda a, b: a + b, x) for x in near]

        def spread(parts):
            return [stack([x * m for m in spots[SMALL]]) for x in parts]

        solved = [unit + x.astype(F32) for x in power]
        power = [x.astype(BF16) for x in each(power, [stack(x) for x in near])]
        size = 4
        while size < SMALL:
            joint = each([stack((x.astype(BF16), y)) for x, y in zip(solved, power)], spread(power))
            solved = [x + y[:SMALL] for x, y in zip(solved, joint)]
            power = [y[SMALL:].astype(BF16) for y in joint]
            size *= 2
        solved = [(x + y).astype(BF16) for x, y in zip(
            solved, each([x.astype(BF16) for x in solved], spread(power)))]
        size = SMALL
        while size < CHUNK:
            count = CHUNK // size
            empty = jnp.zeros((size, CHUNK), BF16)
            band = [stack([masked(x[i * size:(i + 1) * size], spots[size][i - 1]) if i % 2 else empty
                           for i in range(count)]) for x in system]
            mid = [x.astype(BF16) for x in each(solved, band)]
            if 2 * size == CHUNK:
                solved = [(x.astype(F32) * f).astype(BF16) for x, f in zip(solved, flat)]
            wide = [stack([empty if i % 2 else masked(x, spots[size][i]) for i in range(count)])
                    for x in solved]
            low = [x.astype(BF16) for x in each(mid, wide)]
            solved = [stack((masked(x, evens[size]), masked(x, odds[size]) + y))
                      for x, y in zip(solved, low)]
            size *= 2
        wu = [mm(t, stack((k, v), axis=1)).astype(BF16) for t, k, v in zip(solved, ks, vs)]
        made = [mm(kt, y) for kt, y in zip(turned, wu)]
        states = [None] * PAIR
        for c in range(chunks):
            part = slice(c * CHUNK, (c + 1) * CHUNK)
            for lane_of in range(PAIR):
                head = pair * PAIR + lane_of
                x = made[lane_of * chunks + c]
                wu_ref[head, part] = wu[lane_of * chunks + c]
                step = stack((-x[:, :dim], x[:, dim:]), axis=1)
                if c:
                    now = states[lane_of].astype(BF16)
                    state_ref[head, part] = now
                    states[lane_of] = states[lane_of] + step - mm(x[:, :dim], now)
                else:
                    states[lane_of] = step
        for lane_of in range(PAIR):
            ab_ref[pair * PAIR + lane_of] = states[lane_of]

    def compose(pair):
        for lane_of in range(PAIR):
            head = pair * PAIR + lane_of

            @pl.when(x == 0)
            def _():
                made = ab_ref[head]

                @pl.when(sends_row)
                def _():
                    onward[head] = made.astype(BF16)
                    join(head).start()

                @pl.when(sends_state)
                def _():
                    row_a[head] = made[:, :dim].astype(BF16)
                    row_b[head] = made[:, dim:]

            @pl.when(x > 0)
            def _():
                join(head).wait_recv()
                prior = before[head]
                made = ab_ref[head]
                made = made + prior.astype(F32) + mm(made[:, :dim], prior)

                @pl.when(sends_row)
                def _():
                    onward[head] = made.astype(BF16)
                    join(head).start()

                @pl.when(sends_state)
                def _():
                    row_a[head] = made[:, :dim].astype(BF16)
                    row_b[head] = made[:, dim:]

    def pass_on(pair):
        for lane_of in range(PAIR):
            head = pair * PAIR + lane_of

            @pl.when(z > 0)
            def _():
                move(head, 0).wait_recv()

            @pl.when(sends_state)
            def _():
                state = came[head]
                goes[head] = (row_b[head] + state.astype(F32) + mm(row_a[head], state)).astype(BF16)
                for target in range(blks):
                    move(head, target).start()

    def reads_of(pair):
        for lane_of in range(PAIR):
            head = pair * PAIR + lane_of
            q = conv(0, head, lane_of).astype(BF16)
            for c in range(chunks):
                part = slice(c * CHUNK, (c + 1) * CHUNK)
                scores = jnp.where(col <= row, mm(q[part], keys[head, part]), 0.0)
                near = mm(scores, wu_ref[head, part])
                asks = q[part].astype(F32) - near[:, :dim]
                known = near[:, dim:]
                if c:
                    y = mm(asks, state_ref[head, part])
                    asks = asks + y[:, :dim]
                    known = known + y[:, dim:]
                lead_ref[head, part] = asks.astype(BF16)
                known_ref[head, part] = known

    def finish(pair):
        for lane_of in range(PAIR):
            head = pair * PAIR + lane_of
            prior = before[head]
            state = came[head]
            state = state.astype(F32) + mm(prior[:, :dim], state) + prior[:, dim:].astype(F32)
            out = known_ref[head] + mm(lead_ref[head], state)
            mean_sq = jnp.mean(out * out, axis=-1, keepdims=True)
            out = out * lax.rsqrt(mean_sq + 1e-05) * gain_ref[...]
            o_ref[:, lanes_of(head)] = out.astype(o_ref.dtype)

    def first_part(i, carry):
        maps_of(i)

        @pl.when((i >= x) & (i < x + pairs))
        def _():
            compose(i - x)

        @pl.when(i >= lag)
        def _():
            pass_on(i - lag)
        return carry

    def second_part(i, carry):
        reads_of(i - pairs)

        @pl.when((i >= x) & (i < x + pairs))
        def _():
            compose(i - x)

        @pl.when((i >= lag) & (i < lag + pairs))
        def _():
            pass_on(i - lag)

        @pl.when(lag <= pairs)
        def _():
            finish(i - pairs)

        @pl.when((lag > pairs) & (i >= lag))
        def _():
            finish(i - lag)
        return carry

    def third_part(i, carry):
        @pl.when((i >= x) & (i < x + pairs))
        def _():
            compose(i - x)

        @pl.when(i >= lag)
        def _():
            pass_on(i - lag)
            finish(i - lag)
        return carry

    lax.fori_loop(0, pairs, first_part, 0)
    arrive(0)
    lax.fori_loop(pairs, 2 * pairs, second_part, 0)
    lax.fori_loop(2 * pairs, lag + pairs, third_part, 0)

    @pl.when(has_after)
    def _():
        for which in range(3):
            rim_move(which).wait_send()

    @pl.when(sends_row)
    def _():
        for head in range(heads):
            join(head).wait_send()

    @pl.when(sends_state)
    def _():
        for head in range(heads):
            for target in range(blks):
                move(head, target).wait_send()


def on_device(query_raw, key_raw, value_raw, beta_rate, conv_weight, out_gain):
    rows, width = query_raw.shape
    heads = beta_rate.shape[1]
    dim = width // heads
    taps = conv_weight.shape[1]
    seqs, blks = lax.axis_size("seq"), lax.axis_size("blk")
    far = pl.BlockSpec(memory_space=pltpu.HBM)
    vmem = pl.BlockSpec(memory_space=pltpu.VMEM)
    return pl.pallas_call(
        functools.partial(layer_kernel, seqs, blks, taps),
        name="layer",
        out_shape=jax.ShapeDtypeStruct((rows, width), BF16),
        in_specs=[far] * 6,
        out_specs=vmem,
        scratch_shapes=[
            pltpu.VMEM((3, rows, width), BF16),
            pltpu.VMEM((3, RIM, width), BF16),
            pltpu.VMEM((2 * PAIR, rows + LEAD, dim), F32),
            pltpu.VMEM((heads, rows, dim), BF16),
            pltpu.VMEM((3, taps, width), F32),
            pltpu.VMEM((heads, rows), F32),
            pltpu.VMEM((1, dim), F32),
            pltpu.VMEM((heads, rows, 2 * dim), BF16),
            pltpu.VMEM((heads, rows, 2 * dim), BF16),
            pltpu.VMEM((heads, dim, 2 * dim), F32),
            pltpu.VMEM((heads, rows, dim), BF16),
            pltpu.VMEM((heads, rows, dim), F32),
            pltpu.VMEM((heads, dim, dim), BF16),
            pltpu.VMEM((heads, dim, dim), BF16),
            pltpu.VMEM((heads, dim, 2 * dim), BF16),
            pltpu.VMEM((heads, dim, 2 * dim), BF16),
            pltpu.VMEM((heads, dim, dim), BF16),
            pltpu.VMEM((heads, dim, dim), F32),
            pltpu.SemaphoreType.DMA((3,)),
            pltpu.SemaphoreType.DMA((3,)),
            pltpu.SemaphoreType.DMA((3,)),
            pltpu.SemaphoreType.DMA((3,)),
            pltpu.SemaphoreType.DMA((heads,)),
            pltpu.SemaphoreType.DMA((heads,)),
            pltpu.SemaphoreType.DMA((blks, heads)),
            pltpu.SemaphoreType.DMA((heads,)),
        ],
        compiler_params=pltpu.CompilerParams(
            collective_id=0, has_side_effects=True, vmem_limit_bytes=63 << 20),
    )(query_raw, key_raw, value_raw, conv_weight, beta_rate.T, out_gain.reshape(1, dim))


def solution(mesh):
    placed = (
        P(("groups", "seq", "blk"), "hd"),
        P(("groups", "seq", "blk"), "hd"),
        P(("groups", "seq", "blk"), "hd"),
        P(("groups", "seq", "blk"), "hd"),
        P(None, None, "hd"),
        P(),
    )
    return jax.shard_map(
        on_device,
        mesh=mesh,
        in_specs=placed,
        out_specs=P(("groups", "seq", "blk"), "hd"),
        check_vma=False,
    )
```

```python
import functools

import jax
import jax.numpy as jnp
from jax import lax
from jax.experimental import pallas as pl
from jax.experimental.pallas import tpu as pltpu
from jax.sharding import PartitionSpec as P

F32 = jnp.float32
BF16 = jnp.bfloat16
CHUNK = 128
RIM = 16
LEAD = 8
PAIR = 2
QUAD = 4
SMALL = 16
MESH = pl.DeviceIdType.MESH


def mm(a, b):
    return jnp.dot(a.astype(BF16), b.astype(BF16), preferred_element_type=F32)


def mm_nt(a, b):
    return lax.dot_general(a, b, (((1,), (1,)), ((), ())), preferred_element_type=F32)


def stack(parts, axis=0):
    return jnp.concatenate(parts, axis=axis)


def each(lefts, rights):
    made = []
    for i in range(0, len(lefts), 2):
        rows, cols = lefts[i].shape[0], rights[i].shape[1]
        both = mm(stack(lefts[i:i + 2]), stack(rights[i:i + 2], axis=1))
        made += [both[:rows, :cols], both[rows:, cols:]]
    return made


def layer_kernel(seqs, blks, taps, q_hbm, k_hbm, v_hbm, w_hbm, beta_hbm, gain_hbm, o_ref,
                 raw, rim, pad, keys, kv_ref, system_ref, solved_ref, w_ref, beta_ref, gain_ref, wu_ref,
                 state_ref, ab_ref, lead_ref, known_ref, came, entry, goes, mids, before, onward, row_a, row_b,
                 load_sem, small_sem, rim_send, rim_recv, join_send, join_recv, send_sem, mid_send, recv_sem):
    rows = q_hbm.shape[0]
    heads, dim = ab_ref.shape[0], ab_ref.shape[1]
    chunks = rows // CHUNK
    pairs = heads // PAIR
    total = seqs * blks
    z, x = lax.axis_index("seq"), lax.axis_index("blk")
    end = blks - 1
    here = z * blks + x
    half = pairs // 2
    low = x < blks // 2
    shift = jnp.where(low, 0, half)
    last_z = z == seqs - 1
    below = (z + 1) % seqs
    after = (here + 1) % total
    ahead = (here + total - 1) % total
    after_id = {"seq": after // blks, "blk": after % blks}
    ahead_id = {"seq": ahead // blks, "blk": ahead % blks}
    has_ahead = here > 0
    has_after = here < total - 1
    sources = (q_hbm, k_hbm, v_hbm)
    smalls = ((w_hbm, w_ref), (beta_hbm, beta_ref), (gain_hbm, gain_ref))

    def load(which):
        return pltpu.make_async_copy(sources[which], raw.at[which], load_sem.at[which])

    def load_small(i):
        return pltpu.make_async_copy(smalls[i][0], smalls[i][1], small_sem.at[i])

    def rim_move(which):
        return pltpu.make_async_remote_copy(
            src_ref=sources[which].at[pl.ds(rows - RIM, RIM)], dst_ref=rim.at[which],
            send_sem=rim_send.at[which], recv_sem=rim_recv.at[which],
            device_id=after_id, device_id_type=MESH)

    def join(head, forward):
        step = 1 if forward else blks - 1
        return pltpu.make_async_remote_copy(
            src_ref=onward.at[head], dst_ref=before.at[head],
            send_sem=join_send.at[head], recv_sem=join_recv.at[head],
            device_id={"seq": z, "blk": (x + step) % blks}, device_id_type=MESH)

    def move(head, target):
        return pltpu.make_async_remote_copy(
            src_ref=goes.at[head], dst_ref=came.at[head],
            send_sem=send_sem.at[target, head], recv_sem=recv_sem.at[head],
            device_id={"seq": below, "blk": target}, device_id_type=MESH)

    def hand(head):
        return pltpu.make_async_remote_copy(
            src_ref=mids.at[head], dst_ref=came.at[head],
            send_sem=mid_send.at[head], recv_sem=recv_sem.at[head],
            device_id={"seq": z, "blk": (x + 1) % blks}, device_id_type=MESH)

    barrier = pltpu.get_barrier_semaphore()
    above = (z + seqs - 1) % seqs

    def greet(when, seq, blk):
        @pl.when(when)
        def _():
            pl.semaphore_signal(barrier, inc=1, device_id={"seq": seq, "blk": blk}, device_id_type=MESH)

    greet(x > 0, z, (x + blks - 1) % blks)
    greet(x < end, z, (x + 1) % blks)
    greet(z > 0, above, end)
    if blks > 1:
        greet((z > 0) & (x == 0), above, 0)

    load(1).start()
    load_small(0).start()
    load_small(1).start()
    load(2).start()
    load(0).start()
    load_small(2).start()

    @pl.when(here == 0)
    def _():
        rim[...] = jnp.zeros_like(rim)

    @pl.when(z == 0)
    def _():
        came[:heads // 2] = jnp.zeros_like(came[:heads // 2])

    @pl.when((z == 0) & (x == 0))
    def _():
        came[heads // 2:] = jnp.zeros_like(came[heads // 2:])

    targets = (x > 0).astype(jnp.int32) + (x < end).astype(jnp.int32)
    targets = targets + jnp.where((x == end) & (z < seqs - 1), blks, 0)
    if blks > 1:
        targets = targets + jnp.where((x == 0) & (z < seqs - 1), 1, 0)
    pl.semaphore_wait(barrier, targets)

    @pl.when(has_after)
    def _():
        for which in (1, 2, 0):
            rim_move(which).start()

    def rims(kinds):
        @pl.when(has_ahead)
        def _():
            for which in kinds:
                rim_move(which).wait_recv()

    load_small(0).wait()
    load_small(1).wait()
    load_small(2).wait()
    load(1).wait()
    load(2).wait()

    row = lax.broadcasted_iota(jnp.int32, (CHUNK, CHUNK), 0)
    col = lax.broadcasted_iota(jnp.int32, (CHUNK, CHUNK), 1)
    head_row = lax.broadcasted_iota(jnp.int32, (heads, CHUNK), 0)
    lane = lax.broadcasted_iota(jnp.int32, (SMALL, CHUNK), 1)
    level = lax.broadcasted_iota(jnp.int32, (SMALL, CHUNK), 0)

    def keep(mask):
        return jnp.where(mask, 1.0, 0.0).astype(BF16)

    unit = jnp.where(lane % SMALL == level, 1.0, 0.0)
    spots = {}
    size = SMALL
    while size < CHUNK:
        spots[size] = [keep(lane // size == i) for i in range(CHUNK // size)]
        size *= 2
    evens = {s: keep(lane // s % 2 == 0) for s in spots}
    odds = {s: keep(lane // s % 2 == 1) for s in spots}

    def masked(x, mask):
        return stack([x[i:i + SMALL] * mask for i in range(0, x.shape[0], SMALL)])

    def lanes_of(head):
        return pl.ds(pl.multiple_of(head * dim, dim), dim)

    def conv(which, head, slot, count, begun):
        lanes = lanes_of(head)
        if begun:
            pad[slot, 0:LEAD] = rim[which, RIM - LEAD:RIM, lanes].astype(F32)
        else:
            pad[slot, 0:LEAD] = jnp.zeros((LEAD, dim), F32)
        pad[slot, LEAD:LEAD + count] = raw[which, 0:count, lanes].astype(F32)
        half_sum = None
        for tap in range(taps):
            term = (0.5 * w_ref[which, tap:tap + 1, lanes]) * pad[
                slot, pl.ds(LEAD - taps + 1 + tap, count)]
            half_sum = term if half_sum is None else half_sum + term
        return half_sum + half_sum * jnp.tanh(half_sum)

    def heads_of(j):
        first = (j + shift) % pairs * PAIR
        return [first + i for i in range(PAIR)]

    def parts():
        return [slice(c * CHUNK, (c + 1) * CHUNK) for c in range(chunks)]

    def rates_of(head, part):
        return jnp.sum(jnp.where(head_row == head, beta_ref[:, part], 0.0), axis=0, keepdims=True)

    def quad_of(b):
        first = (b * (QUAD // PAIR) + shift) % pairs * PAIR
        return [first + i for i in range(QUAD)]

    def keys_and_values(head, count, begun, slot):
        k = conv(1, head, 2 * slot, count, begun)
        k = (k * lax.rsqrt(jnp.sum(k * k, axis=-1, keepdims=True) + 1e-06)).astype(BF16)
        v = conv(2, head, 2 * slot + 1, count, begun).astype(BF16)
        kv_ref[head, 0:count] = stack((k, v), axis=1)

    def prepare(b):
        first = (b * (QUAD // PAIR) + shift) % pairs * PAIR

        def one(i, carry):
            keys_and_values(first + i, rows, False, 0)
            return carry

        lax.fori_loop(0, QUAD, one, 0)

    def mend(b):
        for i, head in enumerate(quad_of(b)):
            keys_and_values(head, RIM, True, i % 2)

    def invert(b):
        places = [(head, part) for head in quad_of(b) for part in parts()]
        system = []
        for head, part in places:
            k = kv_ref[head, part, 0:dim]
            keys[head, part] = k.T
            down = jnp.sum(jnp.where(row == col, -rates_of(head, part), 0.0), axis=1, keepdims=True)
            system.append(jnp.where(col < row, down * mm_nt(k, k), 0.0).astype(BF16))
        near = [[x[i * SMALL:(i + 1) * SMALL] * m for i, m in enumerate(spots[SMALL])] for x in system]
        power = [functools.reduce(lambda a, b: a + b, x) for x in near]

        def spread(parts):
            return [stack([x * m for m in spots[SMALL]]) for x in parts]

        solved = [unit + x.astype(F32) for x in power]
        power = [x.astype(BF16) for x in each(power, [stack(x) for x in near])]
        size = 4
        while size < SMALL:
            joint = each([stack((x.astype(BF16), y)) for x, y in zip(solved, power)], spread(power))
            solved = [x + y[:SMALL] for x, y in zip(solved, joint)]
            power = [y[SMALL:].astype(BF16) for y in joint]
            size *= 2
        solved = [(x + y).astype(BF16) for x, y in zip(
            solved, each([x.astype(BF16) for x in solved], spread(power)))]
        size = SMALL
        while size < CHUNK:
            count = CHUNK // size
            empty = jnp.zeros((size, CHUNK), BF16)
            band = [stack([masked(x[i * size:(i + 1) * size], spots[size][i - 1]) if i % 2 else empty
                           for i in range(count)]) for x in system]
            mid = [x.astype(BF16) for x in each(solved, band)]
            if 2 * size == CHUNK:
                solved = [(x.astype(F32) * rates_of(head, part)).astype(BF16)
                          for x, (head, part) in zip(solved, places)]
            wide = [stack([empty if i % 2 else masked(x, spots[size][i]) for i in range(count)])
                    for x in solved]
            under = [x.astype(BF16) for x in each(mid, wide)]
            solved = [stack((masked(x, evens[size]), masked(x, odds[size]) + y))
                      for x, y in zip(solved, under)]
            size *= 2
        for x, (head, part) in zip(solved, places):
            solved_ref[head, part] = x

    def gather(j):
        wu = [[mm(solved_ref[head, part], kv_ref[head, part]).astype(BF16) for part in parts()]
              for head in heads_of(j)]
        made = [[mm(keys[head, part], y) for part, y in zip(parts(), ys)]
                for head, ys in zip(heads_of(j), wu)]
        states = [None] * PAIR
        for c, part in enumerate(parts()):
            for i, head in enumerate(heads_of(j)):
                x = made[i][c]
                wu_ref[head, part] = wu[i][c]
                step = stack((-x[:, :dim], x[:, dim:]), axis=1)
                if c:
                    now = states[i].astype(BF16)
                    state_ref[head, part] = now
                    states[i] = states[i] + step - mm(x[:, :dim], now)
                else:
                    states[i] = step
        for i, head in enumerate(heads_of(j)):
            ab_ref[head] = states[i]

    def forward_of(j):
        return (j < half) == low

    def compose(j):
        ahead_of = forward_of(j)

        def keep_row(head, made):
            row_a[head] = made[:, :dim].astype(BF16)
            row_b[head] = made[:, dim:]

        for head in heads_of(j):
            @pl.when(ahead_of & (x == 0))
            def _():
                if blks > 1:
                    onward[head] = ab_ref[head].astype(BF16)
                    join(head, True).start()
                else:
                    keep_row(head, ab_ref[head])

            @pl.when(ahead_of & (x > 0))
            def _():
                join(head, True).wait_recv()
                prior, own = before[head], ab_ref[head]
                made = own + prior.astype(F32) + mm(own[:, :dim], prior)

                @pl.when(x < end)
                def _():
                    onward[head] = made.astype(BF16)
                    join(head, True).start()

                @pl.when(x == end)
                def _():
                    keep_row(head, made)

            @pl.when(jnp.logical_not(ahead_of) & (x == end))
            def _():
                if blks > 1:
                    onward[head] = ab_ref[head].astype(BF16)
                    join(head, False).start()
                else:
                    keep_row(head, ab_ref[head])

            @pl.when(jnp.logical_not(ahead_of) & (x < end))
            def _():
                join(head, False).wait_recv()
                later, own = before[head], ab_ref[head]
                made = own + later.astype(F32) + mm(later[:, :dim], own)

                @pl.when(x > 0)
                def _():
                    onward[head] = made.astype(BF16)
                    join(head, False).start()

                @pl.when(x == 0)
                def _():
                    keep_row(head, made)

    def pass_on(j):
        ahead_of = forward_of(j)
        back = jnp.logical_not(ahead_of)
        for head in heads_of(j):
            @pl.when((z > 0) | (back & (x > 0)))
            def _():
                move(head, 0).wait_recv()

            @pl.when(((ahead_of & (x == end)) | (back & (x == 0))) & (z < seqs - 1))
            def _():
                state = came[head]
                goes[head] = (row_b[head] + state.astype(F32) + mm(row_a[head], state)).astype(BF16)

                @pl.when(back)
                def _():
                    move(head, 0).start()

                @pl.when(ahead_of)
                def _():
                    for target in reversed(range(blks)):
                        move(head, target).start()

            @pl.when(back & (x < end))
            def _():
                state, own = came[head], ab_ref[head]
                mids[head] = (own[:, dim:] + state.astype(F32) + mm(own[:, :dim], state)).astype(BF16)
                hand(head).start()

    def reads_of(j):
        for i, head in enumerate(heads_of(j)):
            q = conv(0, head, i, rows, True).astype(BF16)
            for c, part in enumerate(parts()):
                scores = jnp.where(col <= row, mm(q[part], keys[head, part]), 0.0)
                near = mm(scores, wu_ref[head, part])
                asks = q[part].astype(F32) - near[:, :dim]
                known = near[:, dim:]
                if c:
                    y = mm(asks, state_ref[head, part])
                    asks = asks + y[:, :dim]
                    known = known + y[:, dim:]
                lead_ref[head, part] = asks.astype(BF16)
                known_ref[head, part] = known

    def finish(j):
        for head in heads_of(j):
            @pl.when(forward_of(j) & (x > 0))
            def _():
                prior, state = before[head], came[head]
                entry[head] = (state.astype(F32) + mm(prior[:, :dim], state)
                               + prior[:, dim:].astype(F32)).astype(BF16)

            @pl.when(jnp.logical_not(forward_of(j) & (x > 0)))
            def _():
                entry[head] = came[head]

            out = known_ref[head] + mm(lead_ref[head], entry[head])
            mean_sq = jnp.mean(out * out, axis=-1, keepdims=True)
            out = out * lax.rsqrt(mean_sq + 1e-05) * gain_ref[...]
            o_ref[:, lanes_of(head)] = out.astype(o_ref.dtype)

    def slot_of(q):
        return jnp.minimum(half * (z - 1), pairs) + q

    def first_part(b, carry):
        prepare(b)

        @pl.when(b == 0)
        def _():
            rims((1, 2))

        mend(b)
        invert(b)

        def join_up(g, carry):
            j = b * (QUAD // PAIR) + g
            gather(j)
            compose(j)

            @pl.when((z == 0) & (j >= half))
            def _():
                pass_on(j)
            return carry

        lax.fori_loop(0, QUAD // PAIR, join_up, 0)
        return carry

    def second_part(i, carry):
        reads_of(i)
        for q in range(half):
            @pl.when((z > 0) & (slot_of(q) == i))
            def _():
                pass_on(half + q)
        return carry

    def third_part(m, carry):
        j = (m + half) % pairs

        @pl.when((m >= half) | ((z > 0) & (half * (z - 1) + m >= pairs)))
        def _():
            pass_on(j)
        finish(j)
        return carry

    lax.fori_loop(0, heads // QUAD, first_part, 0)
    load(0).wait()
    rims((0,))
    lax.fori_loop(0, pairs, second_part, 0)
    lax.fori_loop(0, pairs, third_part, 0)

    @pl.when(has_after)
    def _():
        for which in range(3):
            rim_move(which).wait_send()

    forward = range(heads // 2)
    backward = range(heads // 2, heads)

    @pl.when(x < end)
    def _():
        for head in forward:
            join(head, True).wait_send()
        for head in backward:
            hand(head).wait_send()

    @pl.when(x > 0)
    def _():
        for head in backward:
            join(head, False).wait_send()

    @pl.when((x == end) & (z < seqs - 1))
    def _():
        for head in forward:
            for target in range(blks):
                move(head, target).wait_send()

    @pl.when((x == 0) & (z < seqs - 1))
    def _():
        for head in backward:
            move(head, 0).wait_send()


def on_device(query_raw, key_raw, value_raw, beta_rate, conv_weight, out_gain):
    rows, width = query_raw.shape
    heads = beta_rate.shape[1]
    dim = width // heads
    taps = conv_weight.shape[1]
    seqs, blks = lax.axis_size("seq"), lax.axis_size("blk")
    far = pl.BlockSpec(memory_space=pltpu.HBM)
    vmem = pl.BlockSpec(memory_space=pltpu.VMEM)
    return pl.pallas_call(
        functools.partial(layer_kernel, seqs, blks, taps),
        name="layer",
        out_shape=jax.ShapeDtypeStruct((rows, width), BF16),
        in_specs=[far] * 6,
        out_specs=vmem,
        scratch_shapes=[
            pltpu.VMEM((3, rows, width), BF16),
            pltpu.VMEM((3, RIM, width), BF16),
            pltpu.VMEM((2 * PAIR, rows + LEAD, dim), F32),
            pltpu.VMEM((heads, rows, CHUNK), BF16),
            pltpu.VMEM((heads, rows, 2 * dim), BF16),
            pltpu.VMEM((heads, rows, CHUNK), BF16),
            pltpu.VMEM((heads, rows, CHUNK), BF16),
            pltpu.VMEM((3, taps, width), F32),
            pltpu.VMEM((heads, rows), F32),
            pltpu.VMEM((1, dim), F32),
            pltpu.VMEM((heads, rows, 2 * dim), BF16),
            pltpu.VMEM((heads, rows, 2 * dim), BF16),
            pltpu.VMEM((heads, dim, 2 * dim), F32),
            pltpu.VMEM((heads, rows, dim), BF16),
            pltpu.VMEM((heads, rows, dim), F32),
            pltpu.VMEM((heads, dim, dim), BF16),
            pltpu.VMEM((heads, dim, dim), BF16),
            pltpu.VMEM((heads, dim, dim), BF16),
            pltpu.VMEM((heads, dim, dim), BF16),
            pltpu.VMEM((heads, dim, 2 * dim), BF16),
            pltpu.VMEM((heads, dim, 2 * dim), BF16),
            pltpu.VMEM((heads, dim, dim), BF16),
            pltpu.VMEM((heads, dim, dim), F32),
            pltpu.SemaphoreType.DMA((3,)),
            pltpu.SemaphoreType.DMA((3,)),
            pltpu.SemaphoreType.DMA((3,)),
            pltpu.SemaphoreType.DMA((3,)),
            pltpu.SemaphoreType.DMA((heads,)),
            pltpu.SemaphoreType.DMA((heads,)),
            pltpu.SemaphoreType.DMA((blks, heads)),
            pltpu.SemaphoreType.DMA((heads,)),
            pltpu.SemaphoreType.DMA((heads,)),
        ],
        compiler_params=pltpu.CompilerParams(
            collective_id=0, has_side_effects=True, vmem_limit_bytes=52 << 20),
    )(query_raw, key_raw, value_raw, conv_weight, beta_rate.T, out_gain.reshape(1, dim))


def solution(mesh):
    placed = (
        P(("groups", "seq", "blk"), "hd"),
        P(("groups", "seq", "blk"), "hd"),
        P(("groups", "seq", "blk"), "hd"),
        P(("groups", "seq", "blk"), "hd"),
        P(None, None, "hd"),
        P(),
    )
    return jax.shard_map(
        on_device,
        mesh=mesh,
        in_specs=placed,
        out_specs=P(("groups", "seq", "blk"), "hd"),
        check_vma=False,
    )
```

```python
import functools

import jax
import jax.numpy as jnp
from jax import lax
from jax.experimental import pallas as pl
from jax.experimental.pallas import tpu as pltpu
from jax.sharding import PartitionSpec as P

F32 = jnp.float32
BF16 = jnp.bfloat16
CHUNK = 128
RIM = 16
LEAD = 8
PAIR = 2
QUAD = 4
SMALL = 16
MESH = pl.DeviceIdType.MESH


def mm(a, b):
    return jnp.dot(a.astype(BF16), b.astype(BF16), preferred_element_type=F32)


def mm_nt(a, b):
    return lax.dot_general(a, b, (((1,), (1,)), ((), ())), preferred_element_type=F32)


def stack(parts, axis=0):
    return jnp.concatenate(parts, axis=axis)


def each(lefts, rights):
    made = []
    for i in range(0, len(lefts), 2):
        rows, cols = lefts[i].shape[0], rights[i].shape[1]
        both = mm(stack(lefts[i:i + 2]), stack(rights[i:i + 2], axis=1))
        made += [both[:rows, :cols], both[rows:, cols:]]
    return made


def layer_kernel(seqs, blks, taps, q_hbm, k_hbm, v_hbm, w_hbm, beta_hbm, gain_hbm, o_ref,
                 raw, rim, pad, keys, kv_ref, system_ref, solved_ref, w_ref, beta_ref, gain_ref, wu_ref,
                 state_ref, ab_ref, lead_ref, known_ref, came, entry, goes, mids, before, onward, row_a, row_b,
                 load_sem, small_sem, rim_send, rim_recv, join_send, join_recv, send_sem, mid_send, recv_sem):
    rows = q_hbm.shape[0]
    heads, dim = ab_ref.shape[0], ab_ref.shape[1]
    chunks = rows // CHUNK
    pairs = heads // PAIR
    total = seqs * blks
    z, x = lax.axis_index("seq"), lax.axis_index("blk")
    end = blks - 1
    here = z * blks + x
    half = pairs // 2
    low = x < blks // 2
    shift = jnp.where(low, 0, half)
    last_z = z == seqs - 1
    below = (z + 1) % seqs
    after = (here + 1) % total
    ahead = (here + total - 1) % total
    after_id = {"seq": after // blks, "blk": after % blks}
    ahead_id = {"seq": ahead // blks, "blk": ahead % blks}
    has_ahead = here > 0
    has_after = here < total - 1
    sources = (q_hbm, k_hbm, v_hbm)
    smalls = ((w_hbm, w_ref), (beta_hbm, beta_ref), (gain_hbm, gain_ref))

    def load(which):
        return pltpu.make_async_copy(sources[which], raw.at[which], load_sem.at[which])

    def load_small(i):
        return pltpu.make_async_copy(smalls[i][0], smalls[i][1], small_sem.at[i])

    def rim_move(which):
        return pltpu.make_async_remote_copy(
            src_ref=sources[which].at[pl.ds(rows - RIM, RIM)], dst_ref=rim.at[which],
            send_sem=rim_send.at[which], recv_sem=rim_recv.at[which],
            device_id=after_id, device_id_type=MESH)

    def join(head, forward):
        step = 1 if forward else blks - 1
        return pltpu.make_async_remote_copy(
            src_ref=onward.at[head], dst_ref=before.at[head],
            send_sem=join_send.at[head], recv_sem=join_recv.at[head],
            device_id={"seq": z, "blk": (x + step) % blks}, device_id_type=MESH)

    def move(head, target):
        return pltpu.make_async_remote_copy(
            src_ref=goes.at[head], dst_ref=came.at[head],
            send_sem=send_sem.at[target, head], recv_sem=recv_sem.at[head],
            device_id={"seq": below, "blk": target}, device_id_type=MESH)

    def hand(head):
        return pltpu.make_async_remote_copy(
            src_ref=mids.at[head], dst_ref=came.at[head],
            send_sem=mid_send.at[head], recv_sem=recv_sem.at[head],
            device_id={"seq": z, "blk": (x + 1) % blks}, device_id_type=MESH)

    barrier = pltpu.get_barrier_semaphore()
    above = (z + seqs - 1) % seqs

    def greet(when, seq, blk):
        @pl.when(when)
        def _():
            pl.semaphore_signal(barrier, inc=1, device_id={"seq": seq, "blk": blk}, device_id_type=MESH)

    greet(x > 0, z, (x + blks - 1) % blks)
    greet(x < end, z, (x + 1) % blks)
    greet(z > 0, above, end)
    if blks > 1:
        greet((z > 0) & (x == 0), above, 0)

    load(1).start()
    load_small(0).start()
    load_small(1).start()
    load(2).start()
    load(0).start()
    load_small(2).start()

    @pl.when(here == 0)
    def _():
        rim[...] = jnp.zeros_like(rim)

    @pl.when(z == 0)
    def _():
        came[:heads // 2] = jnp.zeros_like(came[:heads // 2])

    @pl.when((z == 0) & (x == 0))
    def _():
        came[heads // 2:] = jnp.zeros_like(came[heads // 2:])

    targets = (x > 0).astype(jnp.int32) + (x < end).astype(jnp.int32)
    targets = targets + jnp.where((x == end) & (z < seqs - 1), blks, 0)
    if blks > 1:
        targets = targets + jnp.where((x == 0) & (z < seqs - 1), 1, 0)
    pl.semaphore_wait(barrier, targets)

    @pl.when(has_after)
    def _():
        for which in (1, 2, 0):
            rim_move(which).start()

    def rims(kinds):
        @pl.when(has_ahead)
        def _():
            for which in kinds:
                rim_move(which).wait_recv()

    load_small(0).wait()
    load_small(1).wait()
    load_small(2).wait()
    load(1).wait()
    load(2).wait()

    row = lax.broadcasted_iota(jnp.int32, (CHUNK, CHUNK), 0)
    col = lax.broadcasted_iota(jnp.int32, (CHUNK, CHUNK), 1)
    head_row = lax.broadcasted_iota(jnp.int32, (heads, CHUNK), 0)
    lane = lax.broadcasted_iota(jnp.int32, (SMALL, CHUNK), 1)
    level = lax.broadcasted_iota(jnp.int32, (SMALL, CHUNK), 0)

    def keep(mask):
        return jnp.where(mask, 1.0, 0.0).astype(BF16)

    unit = jnp.where(lane % SMALL == level, 1.0, 0.0)
    spots = {}
    size = SMALL
    while size < CHUNK:
        spots[size] = [keep(lane // size == i) for i in range(CHUNK // size)]
        size *= 2
    evens = {s: keep(lane // s % 2 == 0) for s in spots}
    odds = {s: keep(lane // s % 2 == 1) for s in spots}

    def masked(x, mask):
        return stack([x[i:i + SMALL] * mask for i in range(0, x.shape[0], SMALL)])

    def lanes_of(head):
        return pl.ds(pl.multiple_of(head * dim, dim), dim)

    def conv(which, head, slot, count, begun):
        lanes = lanes_of(head)
        if begun:
            pad[slot, 0:LEAD] = rim[which, RIM - LEAD:RIM, lanes].astype(F32)
        else:
            pad[slot, 0:LEAD] = jnp.zeros((LEAD, dim), F32)
        pad[slot, LEAD:LEAD + count] = raw[which, 0:count, lanes].astype(F32)
        half_sum = None
        for tap in range(taps):
            term = (0.5 * w_ref[which, tap:tap + 1, lanes]) * pad[
                slot, pl.ds(LEAD - taps + 1 + tap, count)]
            half_sum = term if half_sum is None else half_sum + term
        return half_sum + half_sum * jnp.tanh(half_sum)

    def heads_of(j):
        first = (j + shift) % pairs * PAIR
        return [first + i for i in range(PAIR)]

    def parts():
        return [slice(c * CHUNK, (c + 1) * CHUNK) for c in range(chunks)]

    def rates_of(head, part):
        return jnp.sum(jnp.where(head_row == head, beta_ref[:, part], 0.0), axis=0, keepdims=True)

    def quad_of(b):
        first = (b * (QUAD // PAIR) + shift) % pairs * PAIR
        return [first + i for i in range(QUAD)]

    def keys_and_values(head, count, begun, slot):
        k = conv(1, head, 2 * slot, count, begun)
        k = (k * lax.rsqrt(jnp.sum(k * k, axis=-1, keepdims=True) + 1e-06)).astype(BF16)
        v = conv(2, head, 2 * slot + 1, count, begun).astype(BF16)
        kv_ref[head, 0:count] = stack((k, v), axis=1)

    def prepare(b):
        first = (b * (QUAD // PAIR) + shift) % pairs * PAIR

        def one(i, carry):
            keys_and_values(first + i, rows, False, 0)
            return carry

        lax.fori_loop(0, QUAD, one, 0)

    def mend(b):
        for i, head in enumerate(quad_of(b)):
            keys_and_values(head, RIM, True, i % 2)

    def invert(b):
        places = [(head, part) for head in quad_of(b) for part in parts()]
        system = []
        for head, part in places:
            k = kv_ref[head, part, 0:dim]
            keys[head, part] = k.T
            down = jnp.sum(jnp.where(row == col, -rates_of(head, part), 0.0), axis=1, keepdims=True)
            system.append(jnp.where(col < row, down * mm_nt(k, k), 0.0).astype(BF16))
        near = [[x[i * SMALL:(i + 1) * SMALL] * m for i, m in enumerate(spots[SMALL])] for x in system]
        power = [functools.reduce(lambda a, b: a + b, x) for x in near]

        def spread(parts):
            return [stack([x * m for m in spots[SMALL]]) for x in parts]

        solved = [unit + x.astype(F32) for x in power]
        power = [x.astype(BF16) for x in each(power, [stack(x) for x in near])]
        size = 4
        while size < SMALL:
            joint = each([stack((x.astype(BF16), y)) for x, y in zip(solved, power)], spread(power))
            solved = [x + y[:SMALL] for x, y in zip(solved, joint)]
            power = [y[SMALL:].astype(BF16) for y in joint]
            size *= 2
        solved = [(x + y).astype(BF16) for x, y in zip(
            solved, each([x.astype(BF16) for x in solved], spread(power)))]
        size = SMALL
        while size < CHUNK:
            count = CHUNK // size
            empty = jnp.zeros((size, CHUNK), BF16)
            band = [stack([masked(x[i * size:(i + 1) * size], spots[size][i - 1]) if i % 2 else empty
                           for i in range(count)]) for x in system]
            mid = [x.astype(BF16) for x in each(solved, band)]
            if 2 * size == CHUNK:
                solved = [(x.astype(F32) * rates_of(head, part)).astype(BF16)
                          for x, (head, part) in zip(solved, places)]
            wide = [stack([empty if i % 2 else masked(x, spots[size][i]) for i in range(count)])
                    for x in solved]
            under = [x.astype(BF16) for x in each(mid, wide)]
            solved = [stack((masked(x, evens[size]), masked(x, odds[size]) + y))
                      for x, y in zip(solved, under)]
            size *= 2
        for x, (head, part) in zip(solved, places):
            solved_ref[head, part] = x

    def gather(b):
        heads_here = quad_of(b)
        places = [(head, part) for head in heads_here for part in parts()]
        wu = [mm(solved_ref[head, part], kv_ref[head, part]).astype(BF16) for head, part in places]
        made = [mm(keys[head, part], y) for y, (head, part) in zip(wu, places)]
        for y, (head, part) in zip(wu, places):
            wu_ref[head, part] = y
        made = [stack((-x[:, :dim], x[:, dim:]), axis=1) for x in made]
        made = [made[i:i + chunks] for i in range(0, len(made), chunks)]

        def follow(laters, earliers):
            small = [x.astype(BF16) for x in earliers]
            return small, [x + y + mm(y[:, :dim], e) for x, y, e in zip(earliers, laters, small)]

        so_far = [x[0] for x in made]
        c = 1
        while c < chunks:
            small, longer = follow([x[c] for x in made], so_far)
            for head, x in zip(heads_here, small):
                state_ref[head, parts()[c]] = x
            so_far = longer
            c += 1
        for head, x in zip(heads_here, so_far):
            ab_ref[head] = x

    def forward_of(j):
        return (j < half) == low

    def compose(j):
        ahead_of = forward_of(j)

        def keep_row(head, made):
            row_a[head] = made[:, :dim].astype(BF16)
            row_b[head] = made[:, dim:]

        for head in heads_of(j):
            @pl.when(ahead_of & (x == 0))
            def _():
                if blks > 1:
                    onward[head] = ab_ref[head].astype(BF16)
                    join(head, True).start()
                else:
                    keep_row(head, ab_ref[head])

            @pl.when(ahead_of & (x > 0))
            def _():
                join(head, True).wait_recv()
                prior, own = before[head], ab_ref[head]
                made = own + prior.astype(F32) + mm(own[:, :dim], prior)

                @pl.when(x < end)
                def _():
                    onward[head] = made.astype(BF16)
                    join(head, True).start()

                @pl.when(x == end)
                def _():
                    keep_row(head, made)

            @pl.when(jnp.logical_not(ahead_of) & (x == end))
            def _():
                if blks > 1:
                    onward[head] = ab_ref[head].astype(BF16)
                    join(head, False).start()
                else:
                    keep_row(head, ab_ref[head])

            @pl.when(jnp.logical_not(ahead_of) & (x < end))
            def _():
                join(head, False).wait_recv()
                later, own = before[head], ab_ref[head]
                made = own + later.astype(F32) + mm(later[:, :dim], own)

                @pl.when(x > 0)
                def _():
                    onward[head] = made.astype(BF16)
                    join(head, False).start()

                @pl.when(x == 0)
                def _():
                    keep_row(head, made)

    def pass_on(j):
        ahead_of = forward_of(j)
        back = jnp.logical_not(ahead_of)
        for head in heads_of(j):
            @pl.when((z > 0) | (back & (x > 0)))
            def _():
                move(head, 0).wait_recv()

            @pl.when(((ahead_of & (x == end)) | (back & (x == 0))) & (z < seqs - 1))
            def _():
                state = came[head]
                goes[head] = (row_b[head] + state.astype(F32) + mm(row_a[head], state)).astype(BF16)

                @pl.when(back)
                def _():
                    move(head, 0).start()

                @pl.when(ahead_of)
                def _():
                    for target in reversed(range(blks)):
                        move(head, target).start()

            @pl.when(back & (x < end))
            def _():
                state, own = came[head], ab_ref[head]
                mids[head] = (own[:, dim:] + state.astype(F32) + mm(own[:, :dim], state)).astype(BF16)
                hand(head).start()

    def reads_of(j):
        heads_here = heads_of(j)
        places = [(head, part) for head in heads_here for part in parts()]
        asked = [conv(0, head, i, rows, True).astype(BF16) for i, head in enumerate(heads_here)]
        asked = [q[part] for q in asked for part in parts()]
        scores = [mm(q, keys[head, part]) for q, (head, part) in zip(asked, places)]
        scores = [jnp.where(col <= row, x, 0.0).astype(BF16) for x in scores]
        near = [mm(x, wu_ref[head, part]) for x, (head, part) in zip(scores, places)]
        asks = [q.astype(F32) - y[:, :dim] for q, y in zip(asked, near)]
        made = [mm(a, state_ref[head, part]) if part.start else None
                for a, (head, part) in zip(asks, places)]
        for a, n, y, (head, part) in zip(asks, near, made, places):
            known = n[:, dim:]
            if y is not None:
                a, known = a + y[:, :dim], known + y[:, dim:]
            lead_ref[head, part] = a.astype(BF16)
            known_ref[head, part] = known

    def finish(j):
        for head in heads_of(j):
            @pl.when(forward_of(j) & (x > 0))
            def _():
                prior, state = before[head], came[head]
                entry[head] = (state.astype(F32) + mm(prior[:, :dim], state)
                               + prior[:, dim:].astype(F32)).astype(BF16)

            @pl.when(jnp.logical_not(forward_of(j) & (x > 0)))
            def _():
                entry[head] = came[head]

            out = known_ref[head] + mm(lead_ref[head], entry[head])
            mean_sq = jnp.mean(out * out, axis=-1, keepdims=True)
            out = out * lax.rsqrt(mean_sq + 1e-05) * gain_ref[...]
            o_ref[:, lanes_of(head)] = out.astype(o_ref.dtype)

    def slot_of(q):
        return jnp.minimum(half * (z - 1), pairs) + q

    def first_part(b, carry):
        prepare(b)

        @pl.when(b == 0)
        def _():
            rims((1, 2))

        mend(b)
        invert(b)

        gather(b)

        def join_up(g, carry):
            j = b * (QUAD // PAIR) + g
            compose(j)

            @pl.when((z == 0) & (j >= half))
            def _():
                pass_on(j)
            return carry

        lax.fori_loop(0, QUAD // PAIR, join_up, 0)
        return carry

    def second_part(i, carry):
        reads_of(i)
        for q in range(half):
            @pl.when((z > 0) & (slot_of(q) == i))
            def _():
                pass_on(half + q)
        return carry

    def third_part(m, carry):
        j = (m + half) % pairs

        @pl.when((m >= half) | ((z > 0) & (half * (z - 1) + m >= pairs)))
        def _():
            pass_on(j)
        finish(j)
        return carry

    lax.fori_loop(0, heads // QUAD, first_part, 0)
    load(0).wait()
    rims((0,))
    lax.fori_loop(0, pairs, second_part, 0)
    lax.fori_loop(0, pairs, third_part, 0)

    @pl.when(has_after)
    def _():
        for which in range(3):
            rim_move(which).wait_send()

    forward = range(heads // 2)
    backward = range(heads // 2, heads)

    @pl.when(x < end)
    def _():
        for head in forward:
            join(head, True).wait_send()
        for head in backward:
            hand(head).wait_send()

    @pl.when(x > 0)
    def _():
        for head in backward:
            join(head, False).wait_send()

    @pl.when((x == end) & (z < seqs - 1))
    def _():
        for head in forward:
            for target in range(blks):
                move(head, target).wait_send()

    @pl.when((x == 0) & (z < seqs - 1))
    def _():
        for head in backward:
            move(head, 0).wait_send()


def on_device(query_raw, key_raw, value_raw, beta_rate, conv_weight, out_gain):
    rows, width = query_raw.shape
    heads = beta_rate.shape[1]
    dim = width // heads
    taps = conv_weight.shape[1]
    seqs, blks = lax.axis_size("seq"), lax.axis_size("blk")
    far = pl.BlockSpec(memory_space=pltpu.HBM)
    vmem = pl.BlockSpec(memory_space=pltpu.VMEM)
    return pl.pallas_call(
        functools.partial(layer_kernel, seqs, blks, taps),
        name="layer",
        out_shape=jax.ShapeDtypeStruct((rows, width), BF16),
        in_specs=[far] * 6,
        out_specs=vmem,
        scratch_shapes=[
            pltpu.VMEM((3, rows, width), BF16),
            pltpu.VMEM((3, RIM, width), BF16),
            pltpu.VMEM((2 * PAIR, rows + LEAD, dim), F32),
            pltpu.VMEM((heads, rows, CHUNK), BF16),
            pltpu.VMEM((heads, rows, 2 * dim), BF16),
            pltpu.VMEM((heads, rows, CHUNK), BF16),
            pltpu.VMEM((heads, rows, CHUNK), BF16),
            pltpu.VMEM((3, taps, width), F32),
            pltpu.VMEM((heads, rows), F32),
            pltpu.VMEM((1, dim), F32),
            pltpu.VMEM((heads, rows, 2 * dim), BF16),
            pltpu.VMEM((heads, rows, 2 * dim), BF16),
            pltpu.VMEM((heads, dim, 2 * dim), F32),
            pltpu.VMEM((heads, rows, dim), BF16),
            pltpu.VMEM((heads, rows, dim), F32),
            pltpu.VMEM((heads, dim, dim), BF16),
            pltpu.VMEM((heads, dim, dim), BF16),
            pltpu.VMEM((heads, dim, dim), BF16),
            pltpu.VMEM((heads, dim, dim), BF16),
            pltpu.VMEM((heads, dim, 2 * dim), BF16),
            pltpu.VMEM((heads, dim, 2 * dim), BF16),
            pltpu.VMEM((heads, dim, dim), BF16),
            pltpu.VMEM((heads, dim, dim), F32),
            pltpu.SemaphoreType.DMA((3,)),
            pltpu.SemaphoreType.DMA((3,)),
            pltpu.SemaphoreType.DMA((3,)),
            pltpu.SemaphoreType.DMA((3,)),
            pltpu.SemaphoreType.DMA((heads,)),
            pltpu.SemaphoreType.DMA((heads,)),
            pltpu.SemaphoreType.DMA((blks, heads)),
            pltpu.SemaphoreType.DMA((heads,)),
            pltpu.SemaphoreType.DMA((heads,)),
        ],
        compiler_params=pltpu.CompilerParams(
            collective_id=0, has_side_effects=True, vmem_limit_bytes=52 << 20),
    )(*(pltpu.with_memory_space_constraint(a, pltpu.HBM) for a in (query_raw, key_raw, value_raw, conv_weight, beta_rate.T, out_gain.reshape(1, dim))))


def solution(mesh):
    placed = (
        P(("groups", "seq", "blk"), "hd"),
        P(("groups", "seq", "blk"), "hd"),
        P(("groups", "seq", "blk"), "hd"),
        P(("groups", "seq", "blk"), "hd"),
        P(None, None, "hd"),
        P(),
    )
    return jax.shard_map(
        on_device,
        mesh=mesh,
        in_specs=placed,
        out_specs=P(("groups", "seq", "blk"), "hd"),
        check_vma=False,
    )
```

```python
import functools

import jax
import jax.numpy as jnp
from jax import lax
from jax.experimental import pallas as pl
from jax.experimental.pallas import tpu as pltpu
from jax.sharding import PartitionSpec as P

F32 = jnp.float32
BF16 = jnp.bfloat16
CHUNK = 128
RIM = 16
LEAD = 8
PAIR = 2
QUAD = 4
OFF = 0
SMALL = 16
MESH = pl.DeviceIdType.MESH


def mm(a, b):
    return jnp.dot(a.astype(BF16), b.astype(BF16), preferred_element_type=F32)


def mm_nt(a, b):
    return lax.dot_general(a, b, (((1,), (1,)), ((), ())), preferred_element_type=F32)


def stack(parts, axis=0):
    return jnp.concatenate(parts, axis=axis)


def each(lefts, rights):
    made = []
    for i in range(0, len(lefts), 2):
        rows, cols = lefts[i].shape[0], rights[i].shape[1]
        both = mm(stack(lefts[i:i + 2]), stack(rights[i:i + 2], axis=1))
        made += [both[:rows, :cols], both[rows:, cols:]]
    return made


def layer_kernel(seqs, blks, taps, q_hbm, k_hbm, v_hbm, w_hbm, beta_hbm, gain_hbm, o_ref,
                 raw, rim, pad, keys, kv_ref, system_ref, solved_ref, w_ref, beta_ref, gain_ref, wu_ref,
                 state_ref, ab_ref, lead_ref, known_ref, came, goes, mids, before, onward, row_a, row_b,
                 load_sem, small_sem, rim_send, rim_recv, join_send, join_recv, send_sem, mid_send, recv_sem):
    rows = q_hbm.shape[0]
    heads, dim = ab_ref.shape[0], ab_ref.shape[1]
    chunks = rows // CHUNK
    pairs = heads // PAIR
    total = seqs * blks
    z, x = lax.axis_index("seq"), lax.axis_index("blk")
    end = blks - 1
    here = z * blks + x
    half = pairs // 2
    low = x < blks // 2
    shift = jnp.where(low, 0, half)
    last_z = z == seqs - 1
    below = (z + 1) % seqs
    after = (here + 1) % total
    ahead = (here + total - 1) % total
    after_id = {"seq": after // blks, "blk": after % blks}
    ahead_id = {"seq": ahead // blks, "blk": ahead % blks}
    has_ahead = here > 0
    has_after = here < total - 1
    sources = (q_hbm, k_hbm, v_hbm)
    smalls = ((w_hbm, w_ref), (beta_hbm, beta_ref), (gain_hbm, gain_ref))

    def load(which):
        return pltpu.make_async_copy(sources[which], raw.at[which], load_sem.at[which])

    def load_small(i):
        return pltpu.make_async_copy(smalls[i][0], smalls[i][1], small_sem.at[i])

    def rim_move(which):
        return pltpu.make_async_remote_copy(
            src_ref=sources[which].at[pl.ds(rows - RIM, RIM)], dst_ref=rim.at[which],
            send_sem=rim_send.at[which], recv_sem=rim_recv.at[which],
            device_id=after_id, device_id_type=MESH)

    def join(head, forward):
        step = 1 if forward else blks - 1
        return pltpu.make_async_remote_copy(
            src_ref=onward.at[head], dst_ref=before.at[head],
            send_sem=join_send.at[head], recv_sem=join_recv.at[head],
            device_id={"seq": z, "blk": (x + step) % blks}, device_id_type=MESH)

    def move(head, target):
        return pltpu.make_async_remote_copy(
            src_ref=goes.at[head], dst_ref=came.at[head],
            send_sem=send_sem.at[target, head], recv_sem=recv_sem.at[head],
            device_id={"seq": below, "blk": target}, device_id_type=MESH)

    def hand(head):
        return pltpu.make_async_remote_copy(
            src_ref=mids.at[head], dst_ref=came.at[head],
            send_sem=mid_send.at[head], recv_sem=recv_sem.at[head],
            device_id={"seq": z, "blk": (x + 1) % blks}, device_id_type=MESH)

    barrier = pltpu.get_barrier_semaphore()
    above = (z + seqs - 1) % seqs

    def greet(when, seq, blk):
        @pl.when(when)
        def _():
            pl.semaphore_signal(barrier, inc=1, device_id={"seq": seq, "blk": blk}, device_id_type=MESH)

    greet(x > 0, z, (x + blks - 1) % blks)
    greet(x < end, z, (x + 1) % blks)
    greet(z > 0, above, end)
    if blks > 1:
        greet((z > 0) & (x == 0), above, 0)

    load(1).start()
    load_small(0).start()
    load_small(1).start()
    load(2).start()
    load(0).start()
    load_small(2).start()

    @pl.when(here == 0)
    def _():
        rim[...] = jnp.zeros_like(rim)

    @pl.when(z == 0)
    def _():
        came[:heads // 2] = jnp.zeros_like(came[:heads // 2])

    @pl.when((z == 0) & (x == 0))
    def _():
        came[heads // 2:] = jnp.zeros_like(came[heads // 2:])

    targets = (x > 0).astype(jnp.int32) + (x < end).astype(jnp.int32)
    targets = targets + jnp.where((x == end) & (z < seqs - 1), blks, 0)
    if blks > 1:
        targets = targets + jnp.where((x == 0) & (z < seqs - 1), 1, 0)
    pl.semaphore_wait(barrier, targets)

    @pl.when(has_after)
    def _():
        for which in (1, 2, 0):
            rim_move(which).start()

    def rims(kinds):
        @pl.when(has_ahead)
        def _():
            for which in kinds:
                rim_move(which).wait_recv()

    load_small(0).wait()
    load_small(1).wait()
    load_small(2).wait()
    load(1).wait()
    load(2).wait()

    row = lax.broadcasted_iota(jnp.int32, (CHUNK, CHUNK), 0)
    col = lax.broadcasted_iota(jnp.int32, (CHUNK, CHUNK), 1)
    head_row = lax.broadcasted_iota(jnp.int32, (heads, CHUNK), 0)
    lane = lax.broadcasted_iota(jnp.int32, (SMALL, CHUNK), 1)
    level = lax.broadcasted_iota(jnp.int32, (SMALL, CHUNK), 0)

    def keep(mask):
        return jnp.where(mask, 1.0, 0.0).astype(BF16)

    unit = jnp.where(lane % SMALL == level, 1.0, 0.0)
    spots = {}
    size = SMALL
    while size < CHUNK:
        spots[size] = [keep(lane // size == i) for i in range(CHUNK // size)]
        size *= 2
    evens = {s: keep(lane // s % 2 == 0) for s in spots}
    odds = {s: keep(lane // s % 2 == 1) for s in spots}

    def masked(x, mask):
        return stack([x[i:i + SMALL] * mask for i in range(0, x.shape[0], SMALL)])

    def lanes_of(head):
        return pl.ds(pl.multiple_of(head * dim, dim), dim)

    def conv(which, head, slot, count, begun):
        lanes = lanes_of(head)
        if begun:
            pad[slot, 0:LEAD] = rim[which, RIM - LEAD:RIM, lanes].astype(F32)
        else:
            pad[slot, 0:LEAD] = jnp.zeros((LEAD, dim), F32)
        pad[slot, LEAD:LEAD + count] = raw[which, 0:count, lanes].astype(F32)
        half_sum = None
        for tap in range(taps):
            term = (0.5 * w_ref[which, tap:tap + 1, lanes]) * pad[
                slot, pl.ds(LEAD - taps + 1 + tap, count)]
            half_sum = term if half_sum is None else half_sum + term
        return half_sum + half_sum * jnp.tanh(half_sum)

    def heads_of(j):
        first = (j + shift) % pairs * PAIR
        return [first + i for i in range(PAIR)]

    def parts():
        return [slice(c * CHUNK, (c + 1) * CHUNK) for c in range(chunks)]

    def rates_of(head, part):
        return jnp.sum(jnp.where(head_row == head, beta_ref[:, part], 0.0), axis=0, keepdims=True)

    def quad_of(b):
        first = (b * (QUAD // PAIR) + shift) % pairs * PAIR
        return [first + i for i in range(QUAD)]

    def keys_and_values(head, count, begun, slot):
        k = conv(1, head, 2 * slot, count, begun)
        k = (k * lax.rsqrt(jnp.sum(k * k, axis=-1, keepdims=True) + 1e-06)).astype(BF16)
        v = conv(2, head, 2 * slot + 1, count, begun).astype(BF16)
        kv_ref[head, 0:count] = stack((k, v), axis=1)

    def prepare(b):
        first = (b * (QUAD // PAIR) + shift) % pairs * PAIR

        def one(i, carry):
            keys_and_values(first + i, rows, False, 0)
            return carry

        lax.fori_loop(0, QUAD, one, 0)

    def mend(b):
        for i, head in enumerate(quad_of(b)):
            keys_and_values(head, RIM, True, i % 2)

    def invert(b):
        places = [(head, part) for head in quad_of(b) for part in parts()]
        system = []
        for head, part in places:
            k = kv_ref[head, part, 0:dim]
            keys[head, part] = k.T
            down = jnp.sum(jnp.where(row == col, -rates_of(head, part), 0.0), axis=1, keepdims=True)
            system.append(jnp.where(col < row, down * mm_nt(k, k), 0.0).astype(BF16))
        near = [[x[i * SMALL:(i + 1) * SMALL] * m for i, m in enumerate(spots[SMALL])] for x in system]
        power = [functools.reduce(lambda a, b: a + b, x) for x in near]

        def spread(parts):
            return [stack([x * m for m in spots[SMALL]]) for x in parts]

        solved = [unit + x.astype(F32) for x in power]
        power = [x.astype(BF16) for x in each(power, [stack(x) for x in near])]
        size = 4
        while size < SMALL:
            joint = each([stack((x.astype(BF16), y)) for x, y in zip(solved, power)], spread(power))
            solved = [x + y[:SMALL] for x, y in zip(solved, joint)]
            power = [y[SMALL:].astype(BF16) for y in joint]
            size *= 2
        solved = [(x + y).astype(BF16) for x, y in zip(
            solved, each([x.astype(BF16) for x in solved], spread(power)))]
        size = SMALL
        while size < CHUNK:
            count = CHUNK // size
            empty = jnp.zeros((size, CHUNK), BF16)
            band = [stack([masked(x[i * size:(i + 1) * size], spots[size][i - 1]) if i % 2 else empty
                           for i in range(count)]) for x in system]
            mid = [x.astype(BF16) for x in each(solved, band)]
            if 2 * size == CHUNK:
                solved = [(x.astype(F32) * rates_of(head, part)).astype(BF16)
                          for x, (head, part) in zip(solved, places)]
            wide = [stack([empty if i % 2 else masked(x, spots[size][i]) for i in range(count)])
                    for x in solved]
            under = [x.astype(BF16) for x in each(mid, wide)]
            solved = [stack((masked(x, evens[size]), masked(x, odds[size]) + y))
                      for x, y in zip(solved, under)]
            size *= 2
        for x, (head, part) in zip(solved, places):
            solved_ref[head, part] = x

    def gather(b):
        heads_here = quad_of(b)
        places = [(head, part) for head in heads_here for part in parts()]
        wu = [mm(solved_ref[head, part], kv_ref[head, part]).astype(BF16) for head, part in places]
        made = [mm(keys[head, part], y) for y, (head, part) in zip(wu, places)]
        for y, (head, part) in zip(wu, places):
            wu_ref[head, part] = y
        made = [stack((-x[:, :dim], x[:, dim:]), axis=1) for x in made]
        made = [made[i:i + chunks] for i in range(0, len(made), chunks)]

        def follow(laters, earliers):
            small = [x.astype(BF16) for x in earliers]
            return small, [x + y + mm(y[:, :dim], e) for x, y, e in zip(earliers, laters, small)]

        so_far = [x[0] for x in made]
        c = 1
        while c < chunks:
            small, longer = follow([x[c] for x in made], so_far)
            for head, x in zip(heads_here, small):
                state_ref[head, parts()[c]] = x
            so_far = longer
            c += 1
        for head, x in zip(heads_here, so_far):
            ab_ref[head] = x

    def forward_of(j):
        return (j < half) == low

    def compose(j):
        ahead_of = forward_of(j)

        def keep_row(head, made):
            row_a[head] = made[:, :dim].astype(BF16)
            row_b[head] = made[:, dim:]

        for head in heads_of(j):
            @pl.when(ahead_of & (x == 0))
            def _():
                if blks > 1:
                    onward[head] = ab_ref[head].astype(BF16)
                    join(head, True).start()
                else:
                    keep_row(head, ab_ref[head])

            @pl.when(ahead_of & (x > 0))
            def _():
                join(head, True).wait_recv()
                prior, own = before[head], ab_ref[head]
                made = own + prior.astype(F32) + mm(own[:, :dim], prior)

                @pl.when(x < end)
                def _():
                    onward[head] = made.astype(BF16)
                    join(head, True).start()

                @pl.when(x == end)
                def _():
                    keep_row(head, made)

            @pl.when(jnp.logical_not(ahead_of) & (x == end))
            def _():
                if blks > 1:
                    onward[head] = ab_ref[head].astype(BF16)
                    join(head, False).start()
                else:
                    keep_row(head, ab_ref[head])

            @pl.when(jnp.logical_not(ahead_of) & (x < end))
            def _():
                join(head, False).wait_recv()
                later, own = before[head], ab_ref[head]
                made = own + later.astype(F32) + mm(later[:, :dim], own)

                @pl.when(x > 0)
                def _():
                    onward[head] = made.astype(BF16)
                    join(head, False).start()

                @pl.when(x == 0)
                def _():
                    keep_row(head, made)

    def pass_on(j):
        ahead_of = forward_of(j)
        back = jnp.logical_not(ahead_of)
        chosen = heads_of(j)
        for head in chosen:
            @pl.when((z > 0) | (back & (x > 0)))
            def _():
                move(head, 0).wait_recv()

            @pl.when(((ahead_of & (x == end)) | (back & (x == 0))) & (z < seqs - 1))
            def _():
                state = came[head]
                goes[head] = (row_b[head] + state.astype(F32) + mm(row_a[head], state)).astype(BF16)

                @pl.when(back)
                def _():
                    move(head, 0).start()

                @pl.when(ahead_of)
                def _():
                    move(head, end).start()

            @pl.when(back & (x < end) & (z == seqs - 1))
            def _():
                over(head)

        @pl.when(back & (x < end) & (z < seqs - 1))
        def _():
            for head in chosen:
                over(head)

        if end:
            @pl.when(ahead_of & (x == end) & (z < seqs - 1))
            def _():
                for head in chosen:
                    for target in range(end):
                        move(head, target).start()

    def over(head):
        state, own = came[head], ab_ref[head]
        mids[head] = (own[:, dim:] + state.astype(F32) + mm(own[:, :dim], state)).astype(BF16)
        hand(head).start()

    def reads_of(j):
        heads_here = heads_of(j)
        places = [(head, part) for head in heads_here for part in parts()]
        asked = [conv(0, head, i, rows, True).astype(BF16) for i, head in enumerate(heads_here)]
        asked = [q[part] for q in asked for part in parts()]
        scores = [mm(q, keys[head, part]) for q, (head, part) in zip(asked, places)]
        scores = [jnp.where(col <= row, x, 0.0).astype(BF16) for x in scores]
        near = [mm(x, wu_ref[head, part]) for x, (head, part) in zip(scores, places)]
        asks = [q.astype(F32) - y[:, :dim] for q, y in zip(asked, near)]
        made = [mm(a, state_ref[head, part]) if part.start else None
                for a, (head, part) in zip(asks, places)]
        for a, n, y, (head, part) in zip(asks, near, made, places):
            known = n[:, dim:]
            if y is not None:
                a, known = a + y[:, :dim], known + y[:, dim:]
            lead_ref[head, part] = a.astype(BF16)
            known_ref[head, part] = known

    def finish(j):
        use = forward_of(j) & (x > 0)
        heads_here = heads_of(j)
        states = []
        for head in heads_here:
            prior = jnp.where(use, before[head].astype(F32), 0.0)
            state = came[head]
            states.append(state.astype(F32) + mm(prior[:, :dim], state) + prior[:, dim:])
        outs = [known_ref[head] + mm(lead_ref[head], state) for head, state in zip(heads_here, states)]
        for head, out in zip(heads_here, outs):
            mean_sq = jnp.mean(out * out, axis=-1, keepdims=True)
            out = out * lax.rsqrt(mean_sq + 1e-05) * gain_ref[...]
            o_ref[:, lanes_of(head)] = out.astype(o_ref.dtype)

    def first_part(b, carry):
        prepare(b)

        @pl.when(b == 0)
        def _():
            rims((1, 2))

        mend(b)
        invert(b)

        gather(b)

        def join_up(g, carry):
            j = b * (QUAD // PAIR) + g
            compose(j)

            @pl.when((z == 0) & (j >= half))
            def _():
                pass_on(j)
            return carry

        lax.fori_loop(0, QUAD // PAIR, join_up, 0)
        return carry

    def slot_of(q):
        return jnp.minimum(half * (z - 1), pairs) + q + OFF

    def second_part(i, carry):
        for q in range(half):
            @pl.when((z > 0) & (slot_of(q) == i))
            def _():
                pass_on(half + q)
        reads_of(i)
        return carry

    def third_part(m, carry):
        j = (m + half) % pairs

        @pl.when((m >= half) | ((z > 0) & (slot_of(m) >= pairs)))
        def _():
            pass_on(j)
        finish(j)
        return carry

    lax.fori_loop(0, heads // QUAD, first_part, 0)
    load(0).wait()
    rims((0,))
    lax.fori_loop(0, pairs, second_part, 0)
    lax.fori_loop(0, pairs, third_part, 0)

    @pl.when(has_after)
    def _():
        for which in range(3):
            rim_move(which).wait_send()

    forward = range(heads // 2)
    backward = range(heads // 2, heads)

    @pl.when(x < end)
    def _():
        for head in forward:
            join(head, True).wait_send()
        for head in backward:
            hand(head).wait_send()

    @pl.when(x > 0)
    def _():
        for head in backward:
            join(head, False).wait_send()

    @pl.when((x == end) & (z < seqs - 1))
    def _():
        for head in forward:
            for target in range(blks):
                move(head, target).wait_send()

    @pl.when((x == 0) & (z < seqs - 1))
    def _():
        for head in backward:
            move(head, 0).wait_send()


def on_device(query_raw, key_raw, value_raw, beta_rate, conv_weight, out_gain):
    rows, width = query_raw.shape
    heads = beta_rate.shape[1]
    dim = width // heads
    taps = conv_weight.shape[1]
    seqs, blks = lax.axis_size("seq"), lax.axis_size("blk")
    far = pl.BlockSpec(memory_space=pltpu.HBM)
    vmem = pl.BlockSpec(memory_space=pltpu.VMEM)
    return pl.pallas_call(
        functools.partial(layer_kernel, seqs, blks, taps),
        name="layer",
        out_shape=jax.ShapeDtypeStruct((rows, width), BF16),
        in_specs=[far] * 6,
        out_specs=vmem,
        scratch_shapes=[
            pltpu.VMEM((3, rows, width), BF16),
            pltpu.VMEM((3, RIM, width), BF16),
            pltpu.VMEM((2 * PAIR, rows + LEAD, dim), F32),
            pltpu.VMEM((heads, rows, CHUNK), BF16),
            pltpu.VMEM((heads, rows, 2 * dim), BF16),
            pltpu.VMEM((heads, rows, CHUNK), BF16),
            pltpu.VMEM((heads, rows, CHUNK), BF16),
            pltpu.VMEM((3, taps, width), F32),
            pltpu.VMEM((heads, rows), F32),
            pltpu.VMEM((1, dim), F32),
            pltpu.VMEM((heads, rows, 2 * dim), BF16),
            pltpu.VMEM((heads, rows, 2 * dim), BF16),
            pltpu.VMEM((heads, dim, 2 * dim), F32),
            pltpu.VMEM((heads, rows, dim), BF16),
            pltpu.VMEM((heads, rows, dim), F32),
            pltpu.VMEM((heads, dim, dim), BF16),
            pltpu.VMEM((heads, dim, dim), BF16),
            pltpu.VMEM((heads, dim, dim), BF16),
            pltpu.VMEM((heads, dim, 2 * dim), BF16),
            pltpu.VMEM((heads, dim, 2 * dim), BF16),
            pltpu.VMEM((heads, dim, dim), BF16),
            pltpu.VMEM((heads, dim, dim), F32),
            pltpu.SemaphoreType.DMA((3,)),
            pltpu.SemaphoreType.DMA((3,)),
            pltpu.SemaphoreType.DMA((3,)),
            pltpu.SemaphoreType.DMA((3,)),
            pltpu.SemaphoreType.DMA((heads,)),
            pltpu.SemaphoreType.DMA((heads,)),
            pltpu.SemaphoreType.DMA((blks, heads)),
            pltpu.SemaphoreType.DMA((heads,)),
            pltpu.SemaphoreType.DMA((heads,)),
        ],
        compiler_params=pltpu.CompilerParams(
            collective_id=0, has_side_effects=True, vmem_limit_bytes=52 << 20),
    )(*(pltpu.with_memory_space_constraint(a, pltpu.HBM) for a in (query_raw, key_raw, value_raw, conv_weight, beta_rate.T, out_gain.reshape(1, dim))))


def solution(mesh):
    placed = (
        P(("groups", "seq", "blk"), "hd"),
        P(("groups", "seq", "blk"), "hd"),
        P(("groups", "seq", "blk"), "hd"),
        P(("groups", "seq", "blk"), "hd"),
        P(None, None, "hd"),
        P(),
    )
    return jax.shard_map(
        on_device,
        mesh=mesh,
        in_specs=placed,
        out_specs=P(("groups", "seq", "blk"), "hd"),
        check_vma=False,
    )
```

```python
import functools

import jax
import jax.numpy as jnp
from jax import lax
from jax.experimental import pallas as pl
from jax.experimental.pallas import tpu as pltpu
from jax.sharding import PartitionSpec as P

F32 = jnp.float32
BF16 = jnp.bfloat16
CHUNK = 128
RIM = 16
LEAD = 8
PAIR = 2
QUAD = 4
SMALL = 16
MESH = pl.DeviceIdType.MESH


def mm(a, b):
    return jnp.dot(a.astype(BF16), b.astype(BF16), preferred_element_type=F32)


def mm_nt(a, b):
    return lax.dot_general(a, b, (((1,), (1,)), ((), ())), preferred_element_type=F32)


def stack(parts, axis=0):
    return jnp.concatenate(parts, axis=axis)


def each(lefts, rights):
    made = []
    if lefts[0].shape[0] > 16:
        return [mm(a, b) for a, b in zip(lefts, rights)]
    for i in range(0, len(lefts), 2):
        rows, cols = lefts[i].shape[0], rights[i].shape[1]
        both = mm(stack(lefts[i:i + 2]), stack(rights[i:i + 2], axis=1))
        made += [both[:rows, :cols], both[rows:, cols:]]
    return made


def layer_kernel(seqs, blks, taps, q_hbm, k_hbm, v_hbm, w_hbm, beta_hbm, gain_hbm, o_ref,
                 raw, rim, pad, keys, kv_ref, system_ref, solved_ref, w_ref, beta_ref, gain_ref, wu_ref,
                 state_ref, ab_ref, lead_ref, known_ref, came, goes, mids, before, onward, row_a, row_b,
                 load_sem, small_sem, rim_send, rim_recv, join_send, join_recv, send_sem, mid_send, recv_sem):
    rows = q_hbm.shape[0]
    heads, dim = ab_ref.shape[0], ab_ref.shape[1]
    chunks = rows // CHUNK
    pairs = heads // PAIR
    total = seqs * blks
    z, x = lax.axis_index("seq"), lax.axis_index("blk")
    end = blks - 1
    here = z * blks + x
    half = pairs // 2
    low = x < blks // 2
    shift = jnp.where(low, 0, half)
    last_z = z == seqs - 1
    below = (z + 1) % seqs
    after = (here + 1) % total
    ahead = (here + total - 1) % total
    after_id = {"seq": after // blks, "blk": after % blks}
    ahead_id = {"seq": ahead // blks, "blk": ahead % blks}
    has_ahead = here > 0
    has_after = here < total - 1
    sources = (q_hbm, k_hbm, v_hbm)
    smalls = ((w_hbm, w_ref), (beta_hbm, beta_ref), (gain_hbm, gain_ref))

    def load(which):
        return pltpu.make_async_copy(sources[which], raw.at[which], load_sem.at[which])

    def load_small(i):
        return pltpu.make_async_copy(smalls[i][0], smalls[i][1], small_sem.at[i])

    def rim_move(which):
        return pltpu.make_async_remote_copy(
            src_ref=sources[which].at[pl.ds(rows - RIM, RIM)], dst_ref=rim.at[which],
            send_sem=rim_send.at[which], recv_sem=rim_recv.at[which],
            device_id=after_id, device_id_type=MESH)

    def join(head, forward):
        step = 1 if forward else blks - 1
        return pltpu.make_async_remote_copy(
            src_ref=onward.at[head], dst_ref=before.at[head],
            send_sem=join_send.at[head], recv_sem=join_recv.at[head],
            device_id={"seq": z, "blk": (x + step) % blks}, device_id_type=MESH)

    def move(head, target):
        return pltpu.make_async_remote_copy(
            src_ref=goes.at[head], dst_ref=came.at[head],
            send_sem=send_sem.at[target, head], recv_sem=recv_sem.at[head],
            device_id={"seq": below, "blk": target}, device_id_type=MESH)

    def hand(head):
        return pltpu.make_async_remote_copy(
            src_ref=mids.at[head], dst_ref=came.at[head],
            send_sem=mid_send.at[head], recv_sem=recv_sem.at[head],
            device_id={"seq": z, "blk": (x + 1) % blks}, device_id_type=MESH)

    barrier = pltpu.get_barrier_semaphore()
    above = (z + seqs - 1) % seqs

    def greet(when, seq, blk):
        @pl.when(when)
        def _():
            pl.semaphore_signal(barrier, inc=1, device_id={"seq": seq, "blk": blk}, device_id_type=MESH)

    greet(x > 0, z, (x + blks - 1) % blks)
    greet(x < end, z, (x + 1) % blks)
    greet(z > 0, above, end)
    if blks > 1:
        greet((z > 0) & (x == 0), above, 0)

    load(1).start()
    load_small(0).start()
    load_small(1).start()
    load(2).start()
    load(0).start()
    load_small(2).start()

    @pl.when(here == 0)
    def _():
        rim[...] = jnp.zeros_like(rim)

    @pl.when(z == 0)
    def _():
        came[:heads // 2] = jnp.zeros_like(came[:heads // 2])

    @pl.when((z == 0) & (x == 0))
    def _():
        came[heads // 2:] = jnp.zeros_like(came[heads // 2:])

    targets = (x > 0).astype(jnp.int32) + (x < end).astype(jnp.int32)
    targets = targets + jnp.where((x == end) & (z < seqs - 1), blks, 0)
    if blks > 1:
        targets = targets + jnp.where((x == 0) & (z < seqs - 1), 1, 0)
    pl.semaphore_wait(barrier, targets)

    @pl.when(has_after)
    def _():
        for which in (1, 2, 0):
            rim_move(which).start()

    def rims(kinds):
        @pl.when(has_ahead)
        def _():
            for which in kinds:
                rim_move(which).wait_recv()

    load_small(0).wait()
    load_small(1).wait()
    load_small(2).wait()
    load(1).wait()
    load(2).wait()

    row = lax.broadcasted_iota(jnp.int32, (CHUNK, CHUNK), 0)
    col = lax.broadcasted_iota(jnp.int32, (CHUNK, CHUNK), 1)
    head_row = lax.broadcasted_iota(jnp.int32, (heads, CHUNK), 0)
    lane = lax.broadcasted_iota(jnp.int32, (SMALL, CHUNK), 1)
    level = lax.broadcasted_iota(jnp.int32, (SMALL, CHUNK), 0)

    def keep(mask):
        return jnp.where(mask, 1.0, 0.0).astype(BF16)

    unit = jnp.where(lane % SMALL == level, 1.0, 0.0)
    spots = {}
    size = SMALL
    while size < CHUNK:
        spots[size] = [keep(lane // size == i) for i in range(CHUNK // size)]
        size *= 2
    evens = {s: keep(lane // s % 2 == 0) for s in spots}
    odds = {s: keep(lane // s % 2 == 1) for s in spots}

    def masked(x, mask):
        return stack([x[i:i + SMALL] * mask for i in range(0, x.shape[0], SMALL)])

    def lanes_of(head):
        return pl.ds(pl.multiple_of(head * dim, dim), dim)

    def conv(which, head, slot, count, begun):
        lanes = lanes_of(head)
        if begun:
            pad[slot, 0:LEAD] = rim[which, RIM - LEAD:RIM, lanes].astype(F32)
        else:
            pad[slot, 0:LEAD] = jnp.zeros((LEAD, dim), F32)
        pad[slot, LEAD:LEAD + count] = raw[which, 0:count, lanes].astype(F32)
        half_sum = None
        for tap in range(taps):
            term = (0.5 * w_ref[which, tap:tap + 1, lanes]) * pad[
                slot, pl.ds(LEAD - taps + 1 + tap, count)]
            half_sum = term if half_sum is None else half_sum + term
        return half_sum + half_sum * jnp.tanh(half_sum)

    def heads_of(j):
        first = (j + shift) % pairs * PAIR
        return [first + i for i in range(PAIR)]

    def parts():
        return [slice(c * CHUNK, (c + 1) * CHUNK) for c in range(chunks)]

    def rates_of(head, part):
        return jnp.sum(jnp.where(head_row == head, beta_ref[:, part], 0.0), axis=0, keepdims=True)

    def quad_of(b):
        first = (b * (QUAD // PAIR) + shift) % pairs * PAIR
        return [first + i for i in range(QUAD)]

    def keys_and_values(head, count, begun, slot):
        k = conv(1, head, 2 * slot, count, begun)
        k = (k * lax.rsqrt(jnp.sum(k * k, axis=-1, keepdims=True) + 1e-06)).astype(BF16)
        v = conv(2, head, 2 * slot + 1, count, begun).astype(BF16)
        kv_ref[head, 0:count] = stack((k, v), axis=1)

    def prepare(b):
        first = (b * (QUAD // PAIR) + shift) % pairs * PAIR

        def one(i, carry):
            keys_and_values(first + i, rows, False, 0)
            return carry

        lax.fori_loop(0, QUAD, one, 0)

    def mend(b):
        for i, head in enumerate(quad_of(b)):
            keys_and_values(head, RIM, True, i % 2)

    def invert(b):
        places = [(head, part) for head in quad_of(b) for part in parts()]
        system = []
        for head, part in places:
            k = kv_ref[head, part, 0:dim]
            keys[head, part] = k.T
            down = jnp.sum(jnp.where(row == col, -rates_of(head, part), 0.0), axis=1, keepdims=True)
            system.append(jnp.where(col < row, down * mm_nt(k, k), 0.0).astype(BF16))
        near = [[x[i * SMALL:(i + 1) * SMALL] * m for i, m in enumerate(spots[SMALL])] for x in system]
        power = [functools.reduce(lambda a, b: a + b, x) for x in near]

        def spread(parts):
            return [stack([x * m for m in spots[SMALL]]) for x in parts]

        solved = [unit + x.astype(F32) for x in power]
        power = [x.astype(BF16) for x in each(power, [stack(x) for x in near])]
        size = 4
        while size < SMALL:
            joint = each([stack((x.astype(BF16), y)) for x, y in zip(solved, power)], spread(power))
            solved = [x + y[:SMALL] for x, y in zip(solved, joint)]
            power = [y[SMALL:].astype(BF16) for y in joint]
            size *= 2
        solved = [(x + y).astype(BF16) for x, y in zip(
            solved, each([x.astype(BF16) for x in solved], spread(power)))]
        size = SMALL
        while size < CHUNK:
            count = CHUNK // size
            empty = jnp.zeros((size, CHUNK), BF16)
            band = [stack([masked(x[i * size:(i + 1) * size], spots[size][i - 1]) if i % 2 else empty
                           for i in range(count)]) for x in system]
            mid = [x.astype(BF16) for x in each(solved, band)]
            if 2 * size == CHUNK:
                solved = [(x.astype(F32) * rates_of(head, part)).astype(BF16)
                          for x, (head, part) in zip(solved, places)]
            wide = [stack([empty if i % 2 else masked(x, spots[size][i]) for i in range(count)])
                    for x in solved]
            under = [x.astype(BF16) for x in each(mid, wide)]
            solved = [stack((masked(x, evens[size]), masked(x, odds[size]) + y))
                      for x, y in zip(solved, under)]
            size *= 2
        for x, (head, part) in zip(solved, places):
            solved_ref[head, part] = x

    def gather(b):
        heads_here = quad_of(b)
        places = [(head, part) for head in heads_here for part in parts()]
        wu = [mm(solved_ref[head, part], kv_ref[head, part]).astype(BF16) for head, part in places]
        made = [mm(keys[head, part], y) for y, (head, part) in zip(wu, places)]
        for y, (head, part) in zip(wu, places):
            wu_ref[head, part] = y
        made = [stack((-x[:, :dim], x[:, dim:]), axis=1) for x in made]
        made = [made[i:i + chunks] for i in range(0, len(made), chunks)]

        def follow(laters, earliers):
            small = [x.astype(BF16) for x in earliers]
            return small, [x + y + mm(y[:, :dim], e) for x, y, e in zip(earliers, laters, small)]

        def record(c, small):
            for head, x in zip(heads_here, small):
                state_ref[head, parts()[c]] = x

        one_of = [[x[c] for x in made] for c in range(chunks)]
        so_far = one_of[0]
        c = 1
        while c < chunks:
            if c + 2 < chunks:
                small, two = follow(one_of[c], so_far)
                _, ahead_two = follow(one_of[c + 2], one_of[c + 1])
                record(c, small)
                small, three = follow(one_of[c + 1], two)
                record(c + 1, small)
                record(c + 2, [x.astype(BF16) for x in three])
                _, so_far = follow(ahead_two, two)
                c += 3
            else:
                small, so_far = follow(one_of[c], so_far)
                record(c, small)
                c += 1
        for head, x in zip(heads_here, so_far):
            ab_ref[head] = x

    def forward_of(j):
        return (j < half) == low

    def compose(j):
        ahead_of = forward_of(j)

        def keep_row(head, made):
            row_a[head] = made[:, :dim].astype(BF16)
            row_b[head] = made[:, dim:]

        for head in heads_of(j):
            @pl.when(ahead_of & (x == 0))
            def _():
                if blks > 1:
                    onward[head] = ab_ref[head].astype(BF16)
                    join(head, True).start()
                else:
                    keep_row(head, ab_ref[head])

            @pl.when(ahead_of & (x > 0))
            def _():
                join(head, True).wait_recv()
                prior, own = before[head], ab_ref[head]
                made = own + prior.astype(F32) + mm(own[:, :dim], prior)

                @pl.when(x < end)
                def _():
                    onward[head] = made.astype(BF16)
                    join(head, True).start()

                @pl.when(x == end)
                def _():
                    keep_row(head, made)

            @pl.when(jnp.logical_not(ahead_of) & (x == end))
            def _():
                if blks > 1:
                    onward[head] = ab_ref[head].astype(BF16)
                    join(head, False).start()
                else:
                    keep_row(head, ab_ref[head])

            @pl.when(jnp.logical_not(ahead_of) & (x < end))
            def _():
                join(head, False).wait_recv()
                later, own = before[head], ab_ref[head]
                made = own + later.astype(F32) + mm(later[:, :dim], own)

                @pl.when(x > 0)
                def _():
                    onward[head] = made.astype(BF16)
                    join(head, False).start()

                @pl.when(x == 0)
                def _():
                    keep_row(head, made)

    def pass_on(j):
        ahead_of = forward_of(j)
        back = jnp.logical_not(ahead_of)
        chosen = heads_of(j)
        for head in chosen:
            @pl.when((z > 0) | (back & (x > 0)))
            def _():
                move(head, 0).wait_recv()

            @pl.when(((ahead_of & (x == end)) | (back & (x == 0))) & (z < seqs - 1))
            def _():
                state = came[head]
                goes[head] = (row_b[head] + state.astype(F32) + mm(row_a[head], state)).astype(BF16)

                @pl.when(back)
                def _():
                    move(head, 0).start()

                @pl.when(ahead_of)
                def _():
                    move(head, end).start()

            @pl.when(back & (x < end) & (z == seqs - 1))
            def _():
                over(head)

        @pl.when(back & (x < end) & (z < seqs - 1))
        def _():
            for head in chosen:
                over(head)

        if end:
            @pl.when(ahead_of & (x == end) & (z < seqs - 1))
            def _():
                for head in chosen:
                    for target in range(end):
                        move(head, target).start()

    def over(head):
        state, own = came[head], ab_ref[head]
        mids[head] = (own[:, dim:] + state.astype(F32) + mm(own[:, :dim], state)).astype(BF16)
        hand(head).start()

    def reads_of(j):
        heads_here = heads_of(j)
        places = [(head, part) for head in heads_here for part in parts()]
        asked = [conv(0, head, i, rows, True).astype(BF16) for i, head in enumerate(heads_here)]
        asked = [q[part] for q in asked for part in parts()]
        scores = [mm(q, keys[head, part]) for q, (head, part) in zip(asked, places)]
        scores = [jnp.where(col <= row, x, 0.0).astype(BF16) for x in scores]
        near = [mm(x, wu_ref[head, part]) for x, (head, part) in zip(scores, places)]
        asks = [q.astype(F32) - y[:, :dim] for q, y in zip(asked, near)]
        made = [mm(a, state_ref[head, part]) if part.start else None
                for a, (head, part) in zip(asks, places)]
        for a, n, y, (head, part) in zip(asks, near, made, places):
            known = n[:, dim:]
            if y is not None:
                a, known = a + y[:, :dim], known + y[:, dim:]
            lead_ref[head, part] = a.astype(BF16)
            known_ref[head, part] = known

    def finish(j):
        use = forward_of(j) & (x > 0)
        heads_here = heads_of(j)
        states = []
        for head in heads_here:
            prior = jnp.where(use, before[head].astype(F32), 0.0)
            state = came[head]
            states.append(state.astype(F32) + mm(prior[:, :dim], state) + prior[:, dim:])
        outs = [known_ref[head] + mm(lead_ref[head], state) for head, state in zip(heads_here, states)]
        for head, out in zip(heads_here, outs):
            mean_sq = jnp.mean(out * out, axis=-1, keepdims=True)
            out = out * lax.rsqrt(mean_sq + 1e-05) * gain_ref[...]
            o_ref[:, lanes_of(head)] = out.astype(o_ref.dtype)

    def first_part(b, carry):
        prepare(b)

        @pl.when(b == 0)
        def _():
            rims((1, 2))

        mend(b)
        invert(b)

        gather(b)

        def join_up(g, carry):
            j = b * (QUAD // PAIR) + g
            compose(j)

            @pl.when((z == 0) & (j >= half))
            def _():
                pass_on(j)
            return carry

        lax.fori_loop(0, QUAD // PAIR, join_up, 0)
        return carry

    def slot_of(q):
        return jnp.where(z == 1, 0, jnp.minimum(half * (z - 1), pairs) + q)

    def second_part(i, carry):
        for q in range(half):
            @pl.when((z > 0) & (slot_of(q) == i))
            def _():
                pass_on(half + q)
        reads_of(i)
        return carry

    def third_part(m, carry):
        j = (m + half) % pairs

        @pl.when((m >= half) | ((z > 0) & (slot_of(m) >= pairs)))
        def _():
            pass_on(j)
        finish(j)
        return carry

    lax.fori_loop(0, heads // QUAD, first_part, 0)
    load(0).wait()
    rims((0,))
    lax.fori_loop(0, pairs, second_part, 0)
    lax.fori_loop(0, pairs, third_part, 0)

    @pl.when(has_after)
    def _():
        for which in range(3):
            rim_move(which).wait_send()

    forward = range(heads // 2)
    backward = range(heads // 2, heads)

    @pl.when(x < end)
    def _():
        for head in forward:
            join(head, True).wait_send()
        for head in backward:
            hand(head).wait_send()

    @pl.when(x > 0)
    def _():
        for head in backward:
            join(head, False).wait_send()

    @pl.when((x == end) & (z < seqs - 1))
    def _():
        for head in forward:
            for target in range(blks):
                move(head, target).wait_send()

    @pl.when((x == 0) & (z < seqs - 1))
    def _():
        for head in backward:
            move(head, 0).wait_send()


def on_device(query_raw, key_raw, value_raw, beta_rate, conv_weight, out_gain):
    rows, width = query_raw.shape
    heads = beta_rate.shape[1]
    dim = width // heads
    taps = conv_weight.shape[1]
    seqs, blks = lax.axis_size("seq"), lax.axis_size("blk")
    far = pl.BlockSpec(memory_space=pltpu.HBM)
    vmem = pl.BlockSpec(memory_space=pltpu.VMEM)
    return pl.pallas_call(
        functools.partial(layer_kernel, seqs, blks, taps),
        name="layer",
        out_shape=jax.ShapeDtypeStruct((rows, width), BF16),
        in_specs=[far] * 6,
        out_specs=vmem,
        scratch_shapes=[
            pltpu.VMEM((3, rows, width), BF16),
            pltpu.VMEM((3, RIM, width), BF16),
            pltpu.VMEM((2 * PAIR, rows + LEAD, dim), F32),
            pltpu.VMEM((heads, rows, CHUNK), BF16),
            pltpu.VMEM((heads, rows, 2 * dim), BF16),
            pltpu.VMEM((heads, rows, CHUNK), BF16),
            pltpu.VMEM((heads, rows, CHUNK), BF16),
            pltpu.VMEM((3, taps, width), F32),
            pltpu.VMEM((heads, rows), F32),
            pltpu.VMEM((1, dim), F32),
            pltpu.VMEM((heads, rows, 2 * dim), BF16),
            pltpu.VMEM((heads, rows, 2 * dim), BF16),
            pltpu.VMEM((heads, dim, 2 * dim), F32),
            pltpu.VMEM((heads, rows, dim), BF16),
            pltpu.VMEM((heads, rows, dim), F32),
            pltpu.VMEM((heads, dim, dim), BF16),
            pltpu.VMEM((heads, dim, dim), BF16),
            pltpu.VMEM((heads, dim, dim), BF16),
            pltpu.VMEM((heads, dim, 2 * dim), BF16),
            pltpu.VMEM((heads, dim, 2 * dim), BF16),
            pltpu.VMEM((heads, dim, dim), BF16),
            pltpu.VMEM((heads, dim, dim), F32),
            pltpu.SemaphoreType.DMA((3,)),
            pltpu.SemaphoreType.DMA((3,)),
            pltpu.SemaphoreType.DMA((3,)),
            pltpu.SemaphoreType.DMA((3,)),
            pltpu.SemaphoreType.DMA((heads,)),
            pltpu.SemaphoreType.DMA((heads,)),
            pltpu.SemaphoreType.DMA((blks, heads)),
            pltpu.SemaphoreType.DMA((heads,)),
            pltpu.SemaphoreType.DMA((heads,)),
        ],
        compiler_params=pltpu.CompilerParams(
            collective_id=0, has_side_effects=True, vmem_limit_bytes=52 << 20),
    )(*(pltpu.with_memory_space_constraint(a, pltpu.HBM) for a in (query_raw, key_raw, value_raw, conv_weight, beta_rate.T, out_gain.reshape(1, dim))))


def solution(mesh):
    placed = (
        P(("groups", "seq", "blk"), "hd"),
        P(("groups", "seq", "blk"), "hd"),
        P(("groups", "seq", "blk"), "hd"),
        P(("groups", "seq", "blk"), "hd"),
        P(None, None, "hd"),
        P(),
    )
    return jax.shard_map(
        on_device,
        mesh=mesh,
        in_specs=placed,
        out_specs=P(("groups", "seq", "blk"), "hd"),
        check_vma=False,
    )
```

```python
import functools

import jax
import jax.numpy as jnp
from jax import lax
from jax.experimental import pallas as pl
from jax.experimental.pallas import tpu as pltpu
from jax.sharding import PartitionSpec as P

F32 = jnp.float32
BF16 = jnp.bfloat16
CHUNK = 128
RIM = 16
LEAD = 8
PAIR = 2
QUAD = 4
SMALL = 16
MESH = pl.DeviceIdType.MESH


def mm(a, b):
    return jnp.dot(a.astype(BF16), b.astype(BF16), preferred_element_type=F32)


def mm_nt(a, b):
    return lax.dot_general(a, b, (((1,), (1,)), ((), ())), preferred_element_type=F32)


def stack(parts, axis=0):
    return jnp.concatenate(parts, axis=axis)


def each(lefts, rights):
    made = []
    if lefts[0].shape[0] > 16:
        return [mm(a, b) for a, b in zip(lefts, rights)]
    for i in range(0, len(lefts), 2):
        rows, cols = lefts[i].shape[0], rights[i].shape[1]
        both = mm(stack(lefts[i:i + 2]), stack(rights[i:i + 2], axis=1))
        made += [both[:rows, :cols], both[rows:, cols:]]
    return made


def layer_kernel(seqs, blks, taps, q_hbm, k_hbm, v_hbm, w_hbm, beta_hbm, gain_hbm, o_ref,
                 raw, rim, pad, keys, kv_ref, system_ref, solved_ref, w_ref, beta_ref, gain_ref, wu_ref,
                 state_ref, ab_ref, lead_ref, known_ref, came, goes, mids, before, onward, row_a, row_b,
                 load_sem, small_sem, rim_send, rim_recv, join_send, join_recv, send_sem, mid_send, recv_sem):
    rows = q_hbm.shape[0]
    heads, dim = ab_ref.shape[0], ab_ref.shape[1]
    chunks = rows // CHUNK
    pairs = heads // PAIR
    total = seqs * blks
    z, x = lax.axis_index("seq"), lax.axis_index("blk")
    end = blks - 1
    here = z * blks + x
    half = pairs // 2
    low = x < blks // 2
    shift = jnp.where(low, 0, half)
    last_z = z == seqs - 1
    short = blks == 2 and seqs > 1
    below = (z + 1) % seqs
    after = (here + 1) % total
    ahead = (here + total - 1) % total
    after_id = {"seq": after // blks, "blk": after % blks}
    ahead_id = {"seq": ahead // blks, "blk": ahead % blks}
    has_ahead = here > 0
    has_after = here < total - 1
    sources = (q_hbm, k_hbm, v_hbm)
    smalls = ((w_hbm, w_ref), (beta_hbm, beta_ref), (gain_hbm, gain_ref))

    def load(which):
        return pltpu.make_async_copy(sources[which], raw.at[which], load_sem.at[which])

    def load_small(i):
        return pltpu.make_async_copy(smalls[i][0], smalls[i][1], small_sem.at[i])

    def rim_move(which):
        return pltpu.make_async_remote_copy(
            src_ref=sources[which].at[pl.ds(rows - RIM, RIM)], dst_ref=rim.at[which],
            send_sem=rim_send.at[which], recv_sem=rim_recv.at[which],
            device_id=after_id, device_id_type=MESH)

    def join(head, forward):
        step = 1 if forward else blks - 1
        return pltpu.make_async_remote_copy(
            src_ref=onward.at[head], dst_ref=before.at[head],
            send_sem=join_send.at[head], recv_sem=join_recv.at[head],
            device_id={"seq": z, "blk": (x + step) % blks}, device_id_type=MESH)

    def move(head, target):
        return pltpu.make_async_remote_copy(
            src_ref=goes.at[head], dst_ref=came.at[head],
            send_sem=send_sem.at[target, head], recv_sem=recv_sem.at[head],
            device_id={"seq": below, "blk": target}, device_id_type=MESH)

    def bring(head):
        return pltpu.make_async_remote_copy(
            src_ref=onward.at[head], dst_ref=before.at[head],
            send_sem=join_send.at[head], recv_sem=join_recv.at[head],
            device_id={"seq": z, "blk": (x + 1) % blks}, device_id_type=MESH)

    def hand(head):
        return pltpu.make_async_remote_copy(
            src_ref=mids.at[head], dst_ref=came.at[head],
            send_sem=mid_send.at[head], recv_sem=recv_sem.at[head],
            device_id={"seq": z, "blk": (x + 1) % blks}, device_id_type=MESH)

    barrier = pltpu.get_barrier_semaphore()
    above = (z + seqs - 1) % seqs

    def greet(when, seq, blk):
        @pl.when(when)
        def _():
            pl.semaphore_signal(barrier, inc=1, device_id={"seq": seq, "blk": blk}, device_id_type=MESH)

    greet(x > 0, z, (x + blks - 1) % blks)
    greet(x < end, z, (x + 1) % blks)
    greet(z > 0, above, end)
    if blks > 1:
        greet((z > 0) & (x == 0), above, 0)
    if short:
        greet(last_z & (x == 1), above, 0)

    load(1).start()
    load_small(0).start()
    load_small(1).start()
    load(2).start()
    load(0).start()
    load_small(2).start()

    @pl.when(here == 0)
    def _():
        rim[...] = jnp.zeros_like(rim)

    @pl.when(z == 0)
    def _():
        came[:heads // 2] = jnp.zeros_like(came[:heads // 2])

    @pl.when((z == 0) & (x == 0))
    def _():
        came[heads // 2:] = jnp.zeros_like(came[heads // 2:])

    targets = (x > 0).astype(jnp.int32) + (x < end).astype(jnp.int32)
    targets = targets + jnp.where((x == end) & (z < seqs - 1), blks, 0)
    if blks > 1:
        targets = targets + jnp.where((x == 0) & (z < seqs - 1), 1, 0)
    if short:
        targets = targets + jnp.where((x == 0) & (z == seqs - 2), 1, 0)
    pl.semaphore_wait(barrier, targets)

    @pl.when(has_after)
    def _():
        for which in (1, 2, 0):
            rim_move(which).start()

    def rims(kinds):
        @pl.when(has_ahead)
        def _():
            for which in kinds:
                rim_move(which).wait_recv()

    load_small(0).wait()
    load_small(1).wait()
    load_small(2).wait()
    load(1).wait()
    load(2).wait()

    row = lax.broadcasted_iota(jnp.int32, (CHUNK, CHUNK), 0)
    col = lax.broadcasted_iota(jnp.int32, (CHUNK, CHUNK), 1)
    head_row = lax.broadcasted_iota(jnp.int32, (heads, CHUNK), 0)
    lane = lax.broadcasted_iota(jnp.int32, (SMALL, CHUNK), 1)
    level = lax.broadcasted_iota(jnp.int32, (SMALL, CHUNK), 0)

    def keep(mask):
        return jnp.where(mask, 1.0, 0.0).astype(BF16)

    unit = jnp.where(lane % SMALL == level, 1.0, 0.0)
    spots = {}
    size = SMALL
    while size < CHUNK:
        spots[size] = [keep(lane // size == i) for i in range(CHUNK // size)]
        size *= 2
    evens = {s: keep(lane // s % 2 == 0) for s in spots}
    odds = {s: keep(lane // s % 2 == 1) for s in spots}

    def masked(x, mask):
        return stack([x[i:i + SMALL] * mask for i in range(0, x.shape[0], SMALL)])

    def lanes_of(head):
        return pl.ds(pl.multiple_of(head * dim, dim), dim)

    def conv(which, head, slot, count, begun):
        lanes = lanes_of(head)
        if begun:
            pad[slot, 0:LEAD] = rim[which, RIM - LEAD:RIM, lanes].astype(F32)
        else:
            pad[slot, 0:LEAD] = jnp.zeros((LEAD, dim), F32)
        pad[slot, LEAD:LEAD + count] = raw[which, 0:count, lanes].astype(F32)
        half_sum = None
        for tap in range(taps):
            term = (0.5 * w_ref[which, tap:tap + 1, lanes]) * pad[
                slot, pl.ds(LEAD - taps + 1 + tap, count)]
            half_sum = term if half_sum is None else half_sum + term
        return half_sum + half_sum * jnp.tanh(half_sum)

    def heads_of(j):
        first = (j + shift) % pairs * PAIR
        return [first + i for i in range(PAIR)]

    def parts():
        return [slice(c * CHUNK, (c + 1) * CHUNK) for c in range(chunks)]

    def rates_of(head, part):
        return jnp.sum(jnp.where(head_row == head, beta_ref[:, part], 0.0), axis=0, keepdims=True)

    def quad_of(b):
        first = (b * (QUAD // PAIR) + shift) % pairs * PAIR
        return [first + i for i in range(QUAD)]

    def keys_and_values(head, count, begun, slot):
        k = conv(1, head, 2 * slot, count, begun)
        k = (k * lax.rsqrt(jnp.sum(k * k, axis=-1, keepdims=True) + 1e-06)).astype(BF16)
        v = conv(2, head, 2 * slot + 1, count, begun).astype(BF16)
        kv_ref[head, 0:count] = stack((k, v), axis=1)

    def prepare(b):
        first = (b * (QUAD // PAIR) + shift) % pairs * PAIR

        def one(i, carry):
            keys_and_values(first + i, rows, False, 0)
            return carry

        lax.fori_loop(0, QUAD, one, 0)

    def mend(b):
        for i, head in enumerate(quad_of(b)):
            keys_and_values(head, RIM, True, i % 2)

    def invert(b):
        places = [(head, part) for head in quad_of(b) for part in parts()]
        system = []
        for head, part in places:
            k = kv_ref[head, part, 0:dim]
            keys[head, part] = k.T
            down = jnp.sum(jnp.where(row == col, -rates_of(head, part), 0.0), axis=1, keepdims=True)
            system.append(jnp.where(col < row, down * mm_nt(k, k), 0.0).astype(BF16))
        near = [[x[i * SMALL:(i + 1) * SMALL] * m for i, m in enumerate(spots[SMALL])] for x in system]
        power = [functools.reduce(lambda a, b: a + b, x) for x in near]

        def spread(parts):
            return [stack([x * m for m in spots[SMALL]]) for x in parts]

        solved = [unit + x.astype(F32) for x in power]
        power = [x.astype(BF16) for x in each(power, [stack(x) for x in near])]
        size = 4
        while size < SMALL:
            joint = each([stack((x.astype(BF16), y)) for x, y in zip(solved, power)], spread(power))
            solved = [x + y[:SMALL] for x, y in zip(solved, joint)]
            power = [y[SMALL:].astype(BF16) for y in joint]
            size *= 2
        solved = [(x + y).astype(BF16) for x, y in zip(
            solved, each([x.astype(BF16) for x in solved], spread(power)))]
        size = SMALL
        while size < CHUNK:
            count = CHUNK // size
            empty = jnp.zeros((size, CHUNK), BF16)
            band = [stack([masked(x[i * size:(i + 1) * size], spots[size][i - 1]) if i % 2 else empty
                           for i in range(count)]) for x in system]
            mid = [x.astype(BF16) for x in each(solved, band)]
            if 2 * size == CHUNK:
                solved = [(x.astype(F32) * rates_of(head, part)).astype(BF16)
                          for x, (head, part) in zip(solved, places)]
            wide = [stack([empty if i % 2 else masked(x, spots[size][i]) for i in range(count)])
                    for x in solved]
            under = [x.astype(BF16) for x in each(mid, wide)]
            solved = [stack((masked(x, evens[size]), masked(x, odds[size]) + y))
                      for x, y in zip(solved, under)]
            size *= 2
        for x, (head, part) in zip(solved, places):
            solved_ref[head, part] = x

    def gather(b):
        heads_here = quad_of(b)
        places = [(head, part) for head in heads_here for part in parts()]
        wu = [mm(solved_ref[head, part], kv_ref[head, part]).astype(BF16) for head, part in places]
        made = [mm(keys[head, part], y) for y, (head, part) in zip(wu, places)]
        for y, (head, part) in zip(wu, places):
            wu_ref[head, part] = y
        made = [stack((-x[:, :dim], x[:, dim:]), axis=1) for x in made]
        made = [made[i:i + chunks] for i in range(0, len(made), chunks)]

        def follow(laters, earliers):
            small = [x.astype(BF16) for x in earliers]
            return small, [x + y + mm(y[:, :dim], e) for x, y, e in zip(earliers, laters, small)]

        def record(c, small):
            for head, x in zip(heads_here, small):
                state_ref[head, parts()[c]] = x

        one_of = [[x[c] for x in made] for c in range(chunks)]
        so_far = one_of[0]
        c = 1
        while c < chunks:
            if c + 2 < chunks:
                small, two = follow(one_of[c], so_far)
                _, ahead_two = follow(one_of[c + 2], one_of[c + 1])
                record(c, small)
                small, three = follow(one_of[c + 1], two)
                record(c + 1, small)
                record(c + 2, [x.astype(BF16) for x in three])
                _, so_far = follow(ahead_two, two)
                c += 3
            else:
                small, so_far = follow(one_of[c], so_far)
                record(c, small)
                c += 1
        for head, x in zip(heads_here, so_far):
            ab_ref[head] = x

    def forward_of(j):
        return (j < half) == low

    def compose(j):
        ahead_of = forward_of(j)

        def keep_row(head, made):
            row_a[head] = made[:, :dim].astype(BF16)
            row_b[head] = made[:, dim:]

        for head in heads_of(j):
            @pl.when(ahead_of & (x == 0))
            def _():
                if blks > 1:
                    onward[head] = ab_ref[head].astype(BF16)
                    join(head, True).start()
                else:
                    keep_row(head, ab_ref[head])

            @pl.when(ahead_of & (x > 0))
            def _():
                join(head, True).wait_recv()
                prior, own = before[head], ab_ref[head]
                made = own + prior.astype(F32) + mm(own[:, :dim], prior)

                @pl.when(x < end)
                def _():
                    onward[head] = made.astype(BF16)
                    join(head, True).start()

                @pl.when(x == end)
                def _():
                    keep_row(head, made)

            @pl.when(jnp.logical_not(ahead_of) & (x == end))
            def _():
                if blks > 1:
                    onward[head] = ab_ref[head].astype(BF16)
                    join(head, False).start()
                else:
                    keep_row(head, ab_ref[head])

            @pl.when(jnp.logical_not(ahead_of) & (x < end))
            def _():
                join(head, False).wait_recv()
                later, own = before[head], ab_ref[head]
                made = own + later.astype(F32) + mm(later[:, :dim], own)

                @pl.when(x > 0)
                def _():
                    onward[head] = made.astype(BF16)
                    join(head, False).start()

                @pl.when(x == 0)
                def _():
                    keep_row(head, made)

                if short:
                    @pl.when((x == 0) & last_z)
                    def _():
                        onward[head] = own.astype(BF16)
                        bring(head).start()

    def pass_on(j):
        ahead_of = forward_of(j)
        back = jnp.logical_not(ahead_of)
        chosen = heads_of(j)
        for head in chosen:
            @pl.when((z > 0) | (back & (x > 0)))
            def _():
                move(head, 0).wait_recv()

            @pl.when(((ahead_of & (x == end)) | (back & (x == 0))) & (z < seqs - 1))
            def _():
                state = came[head]
                goes[head] = (row_b[head] + state.astype(F32) + mm(row_a[head], state)).astype(BF16)

                @pl.when(back)
                def _():
                    move(head, 0).start()

                    if short:
                        @pl.when(z == seqs - 2)
                        def _():
                            move(head, 1).start()

                @pl.when(ahead_of)
                def _():
                    move(head, end).start()

            if short:
                @pl.when(back & (x == 1) & last_z)
                def _():
                    bring(head).wait_recv()
            else:
                @pl.when(back & (x < end) & (z == seqs - 1))
                def _():
                    over(head)

        @pl.when(back & (x < end) & (z < seqs - 1))
        def _():
            for head in chosen:
                over(head)

        if end:
            @pl.when(ahead_of & (x == end) & (z < seqs - 1))
            def _():
                for head in chosen:
                    for target in range(end):
                        move(head, target).start()

    def over(head):
        state, own = came[head], ab_ref[head]
        mids[head] = (own[:, dim:] + state.astype(F32) + mm(own[:, :dim], state)).astype(BF16)
        hand(head).start()

    def reads_of(j):
        heads_here = heads_of(j)
        places = [(head, part) for head in heads_here for part in parts()]
        asked = [conv(0, head, i, rows, True).astype(BF16) for i, head in enumerate(heads_here)]
        asked = [q[part] for q in asked for part in parts()]
        scores = [mm(q, keys[head, part]) for q, (head, part) in zip(asked, places)]
        scores = [jnp.where(col <= row, x, 0.0).astype(BF16) for x in scores]
        near = [mm(x, wu_ref[head, part]) for x, (head, part) in zip(scores, places)]
        asks = [q.astype(F32) - y[:, :dim] for q, y in zip(asked, near)]
        made = [mm(a, state_ref[head, part]) if part.start else None
                for a, (head, part) in zip(asks, places)]
        for a, n, y, (head, part) in zip(asks, near, made, places):
            known = n[:, dim:]
            if y is not None:
                a, known = a + y[:, :dim], known + y[:, dim:]
            lead_ref[head, part] = a.astype(BF16)
            known_ref[head, part] = known

    def finish(j):
        use = forward_of(j) & (x > 0)
        if short:
            use = use | (jnp.logical_not(forward_of(j)) & (x == 1) & last_z)
        heads_here = heads_of(j)
        states = []
        for head in heads_here:
            prior = jnp.where(use, before[head].astype(F32), 0.0)
            state = came[head]
            states.append(state.astype(F32) + mm(prior[:, :dim], state) + prior[:, dim:])
        outs = [known_ref[head] + mm(lead_ref[head], state) for head, state in zip(heads_here, states)]
        for head, out in zip(heads_here, outs):
            mean_sq = jnp.mean(out * out, axis=-1, keepdims=True)
            out = out * lax.rsqrt(mean_sq + 1e-05) * gain_ref[...]
            o_ref[:, lanes_of(head)] = out.astype(o_ref.dtype)

    def first_part(b, carry):
        prepare(b)

        @pl.when(b == 0)
        def _():
            rims((1, 2))

        mend(b)
        invert(b)

        gather(b)

        def join_up(g, carry):
            j = b * (QUAD // PAIR) + g
            compose(j)

            @pl.when((z == 0) & (j >= half))
            def _():
                pass_on(j)
            return carry

        lax.fori_loop(0, QUAD // PAIR, join_up, 0)
        return carry

    def slot_of(q):
        return jnp.where(z == 1, 0, jnp.minimum(half * (z - 1), pairs) + q)

    def second_part(i, carry):
        for q in range(half):
            @pl.when((z > 0) & (slot_of(q) == i))
            def _():
                pass_on(half + q)
        reads_of(i)
        return carry

    def third_part(m, carry):
        j = (m + half) % pairs

        @pl.when((m >= half) | ((z > 0) & (slot_of(m) >= pairs)))
        def _():
            pass_on(j)
        finish(j)
        return carry

    lax.fori_loop(0, heads // QUAD, first_part, 0)
    load(0).wait()
    rims((0,))
    lax.fori_loop(0, pairs, second_part, 0)
    lax.fori_loop(0, pairs, third_part, 0)

    @pl.when(has_after)
    def _():
        for which in range(3):
            rim_move(which).wait_send()

    forward = range(heads // 2)
    backward = range(heads // 2, heads)

    @pl.when(x < end)
    def _():
        for head in forward:
            join(head, True).wait_send()
        for head in backward:
            if short:
                @pl.when(last_z)
                def _():
                    bring(head).wait_send()

                @pl.when(jnp.logical_not(last_z))
                def _():
                    hand(head).wait_send()
            else:
                hand(head).wait_send()

    @pl.when(x > 0)
    def _():
        for head in backward:
            join(head, False).wait_send()

    @pl.when((x == end) & (z < seqs - 1))
    def _():
        for head in forward:
            for target in range(blks):
                move(head, target).wait_send()

    @pl.when((x == 0) & (z < seqs - 1))
    def _():
        for head in backward:
            move(head, 0).wait_send()
            if short:
                @pl.when(z == seqs - 2)
                def _():
                    move(head, 1).wait_send()


def on_device(query_raw, key_raw, value_raw, beta_rate, conv_weight, out_gain):
    rows, width = query_raw.shape
    heads = beta_rate.shape[1]
    dim = width // heads
    taps = conv_weight.shape[1]
    seqs, blks = lax.axis_size("seq"), lax.axis_size("blk")
    far = pl.BlockSpec(memory_space=pltpu.HBM)
    vmem = pl.BlockSpec(memory_space=pltpu.VMEM)
    return pl.pallas_call(
        functools.partial(layer_kernel, seqs, blks, taps),
        name="layer",
        out_shape=jax.ShapeDtypeStruct((rows, width), BF16),
        in_specs=[far] * 6,
        out_specs=vmem,
        scratch_shapes=[
            pltpu.VMEM((3, rows, width), BF16),
            pltpu.VMEM((3, RIM, width), BF16),
            pltpu.VMEM((2 * PAIR, rows + LEAD, dim), F32),
            pltpu.VMEM((heads, rows, CHUNK), BF16),
            pltpu.VMEM((heads, rows, 2 * dim), BF16),
            pltpu.VMEM((heads, rows, CHUNK), BF16),
            pltpu.VMEM((heads, rows, CHUNK), BF16),
            pltpu.VMEM((3, taps, width), F32),
            pltpu.VMEM((heads, rows), F32),
            pltpu.VMEM((1, dim), F32),
            pltpu.VMEM((heads, rows, 2 * dim), BF16),
            pltpu.VMEM((heads, rows, 2 * dim), BF16),
            pltpu.VMEM((heads, dim, 2 * dim), F32),
            pltpu.VMEM((heads, rows, dim), BF16),
            pltpu.VMEM((heads, rows, dim), F32),
            pltpu.VMEM((heads, dim, dim), BF16),
            pltpu.VMEM((heads, dim, dim), BF16),
            pltpu.VMEM((heads, dim, dim), BF16),
            pltpu.VMEM((heads, dim, 2 * dim), BF16),
            pltpu.VMEM((heads, dim, 2 * dim), BF16),
            pltpu.VMEM((heads, dim, dim), BF16),
            pltpu.VMEM((heads, dim, dim), F32),
            pltpu.SemaphoreType.DMA((3,)),
            pltpu.SemaphoreType.DMA((3,)),
            pltpu.SemaphoreType.DMA((3,)),
            pltpu.SemaphoreType.DMA((3,)),
            pltpu.SemaphoreType.DMA((heads,)),
            pltpu.SemaphoreType.DMA((heads,)),
            pltpu.SemaphoreType.DMA((blks, heads)),
            pltpu.SemaphoreType.DMA((heads,)),
            pltpu.SemaphoreType.DMA((heads,)),
        ],
        compiler_params=pltpu.CompilerParams(
            collective_id=0, has_side_effects=True, vmem_limit_bytes=52 << 20),
    )(*(pltpu.with_memory_space_constraint(a, pltpu.HBM) for a in (query_raw, key_raw, value_raw, conv_weight, beta_rate.T, out_gain.reshape(1, dim))))


def solution(mesh):
    placed = (
        P(("groups", "seq", "blk"), "hd"),
        P(("groups", "seq", "blk"), "hd"),
        P(("groups", "seq", "blk"), "hd"),
        P(("groups", "seq", "blk"), "hd"),
        P(None, None, "hd"),
        P(),
    )
    return jax.shard_map(
        on_device,
        mesh=mesh,
        in_specs=placed,
        out_specs=P(("groups", "seq", "blk"), "hd"),
        check_vma=False,
    )
```
